256 devices in a mesh: rows: 16 (over z_hi, x, core), feat: 16 (over y, z_lo).
Axes of the slice: x: 4, y: 4, z: 8 (z_hi: 2, z_lo: 4; z = z_hi * 4 + z_lo), core: 2. Of those that a mesh axis runs over, the one named last changes fastest.
Arguments:
- design: bfloat16 [12288, 65536], P('rows', 'feat'), may hold values from -0.0234375 to 0.0234375
- labels: int32 [64, 12288], P(None, 'rows'), may hold values from -1 to 1, as said below
- local_x: float32 [16, 64, 65536], P('rows', None, 'feat'), may hold values from -6 to 6
- dual_u: float32 [16, 64, 65536], P('rows', None, 'feat'), may hold values from -3 to 3
- consensus_z: float32 [64, 65536], P(None, 'feat'), may hold values from -6 to 6
- step_size: float32 [64], replicated, may hold values from 0.5 to 1
- rho: float32 [64], replicated, may hold values from 0.5 to 1.5
- penalty: float32 [64], replicated, may hold values from 0.5 to 4
Outputs:
- new_x: float32 [16, 64, 65536], P('rows', None, 'feat')
- new_z: float32 [64, 65536], P(None, 'feat')
- new_u: float32 [16, 64, 65536], P('rows', None, 'feat')
The draws below stay inside these ranges and needn't reach their ends.
Inputs may be any that keep to these rules, and one draw needn't show every extreme that they name: `labels`: each entry is -1 or 1.
All inputs are finite; a program needn't handle non-finite values.
Results may differ from the reference program's by a relative error of at most 0.0023.
Values may be sent and summed in bfloat16 or wider, within the bound.
A program may use at most 64 MiB of HBM per device.

```python
import math
import jax
import jax.numpy as jnp
from jax import lax

F = 65536
K = 64
S_DEV = 768
SAMPLES = 12288
BLOCKS = 16
N_ROWS = 16


def draw_labels(key, part):
    return (2 * jax.random.randint(key, (K, SAMPLES), 0, 2) - 1).astype(jnp.int32)


def block_levels(stream_key, dims, pieces, smallest, largest):
    def one(position, parts):
        heights = jax.random.uniform(jax.random.fold_in(jax.random.fold_in(stream_key, 6), position), (parts,), jnp.float32, smallest / len(pieces), largest / len(pieces))
        return jnp.repeat(jnp.exp(heights), dims[position] // parts).reshape((-1,) + (1,) * (len(dims) - position - 1))

    factor_of = one(*pieces[0])
    for cut in pieces[1:]:
        factor_of = factor_of * one(*cut)
    return factor_of


def gaussian(key, shape, spread, bound, pieces=(), dtype=jnp.bfloat16):
    level = block_levels(key, shape, pieces, -0.22, 0.18) if pieces else 1.0
    values = jax.random.normal(key, shape, jnp.float32) * spread * level
    return jnp.minimum(jnp.maximum(values, -bound), bound).astype(dtype)


def setup_inputs(seed: int = 0) -> dict:
    seeds = jax.random.split(jax.random.key(seed), 9)
    return {
        "design": gaussian(seeds[0], (SAMPLES, F), (F ** -0.5), 0.0234375, ((0, 16), (1, 16))),
        "labels": draw_labels(jax.random.fold_in(seeds[8], 71), 0),
        "local_x": gaussian(seeds[2], (BLOCKS, K, F), 1.0, 6.0, ((0, 16), (2, 16)), jnp.float32),
        "dual_u": gaussian(seeds[3], (BLOCKS, K, F), 0.5, 3.0, ((0, 16), (2, 16)), jnp.float32),
        "consensus_z": gaussian(seeds[4], (K, F), 1.0, 6.0, ((1, 16),), jnp.float32),
        "step_size": jnp.clip(jnp.exp(jax.random.uniform(seeds[5], (K,), jnp.float32, math.log(0.5), math.log(1.0))), 0.5, 1.0),
        "rho": jnp.clip(jnp.exp(jax.random.uniform(seeds[6], (K,), jnp.float32, math.log(0.5), math.log(1.5))), 0.5, 1.5),
        "penalty": jnp.clip(jnp.exp(jax.random.uniform(seeds[7], (K,), jnp.float32, math.log(0.5), math.log(4.0))), 0.5, 4.0),
    }


def reference(design, labels, local_x, dual_u, consensus_z, step_size, rho, penalty):
    blocks = design.reshape(N_ROWS, S_DEV, F)
    signs = labels.reshape(K, N_ROWS, S_DEV).transpose(1, 0, 2).astype(jnp.float32)
    eta = step_size[:, None]
    weight = rho[:, None]

    def solve(item):
        rows_block, sign, x, u = item
        for turn in range(2):
            xb = x.astype(jnp.bfloat16)
            margin = lax.dot_general(xb, rows_block, (((1,), (1,)), ((), ())), preferred_element_type=jnp.float32)
            resid = (sign * jax.nn.sigmoid(-sign * margin)).astype(jnp.bfloat16)
            grad = jnp.dot(resid, rows_block, preferred_element_type=jnp.float32)
            x = x - eta * (weight * (x - consensus_z + u) - grad)
        return x

    new_x = lax.map(solve, (blocks, signs, local_x, dual_u))
    mean = jnp.sum(new_x + dual_u, axis=0) / N_ROWS
    limit = (penalty / (rho * N_ROWS))[:, None]
    new_z = mean - jnp.clip(mean, -limit, limit)
    new_u = dual_u + new_x - new_z[None]
    return new_x, new_z, new_u
```

```python
import functools

import jax
import jax.numpy as jnp
from jax import lax
from jax.experimental import pallas as pl
from jax.experimental.pallas import tpu as pltpu
from jax.sharding import PartitionSpec as P

MESH = pl.DeviceIdType.MESH
AXES = ("rows", "feat")


def _device(axis, peer):
    return tuple(peer if a == axis else lax.axis_index(a) for a in AXES)


def _allreduce_kernel(axis, n, x_ref, o_ref, recv, gath, ssem1, rsem1, ssem2, rsem2):
    me = lax.axis_index(axis)
    peers = [lax.rem(me + d, n) for d in range(n)]
    srcs = [lax.rem(me + n - d, n) for d in range(n)]

    barrier = pltpu.get_barrier_semaphore()
    for d in range(1, n):
        pl.semaphore_signal(barrier, inc=1, device_id=_device(axis, peers[d]), device_id_type=MESH)
    pl.semaphore_wait(barrier, n - 1)

    sends = []
    for d in range(1, n):
        c = pltpu.make_async_remote_copy(
            src_ref=x_ref.at[peers[d]],
            dst_ref=recv.at[me],
            send_sem=ssem1.at[d],
            recv_sem=rsem1.at[d],
            device_id=_device(axis, peers[d]),
            device_id_type=MESH,
        )
        c.start()
        sends.append(c)
    acc = x_ref[me]
    for d in range(1, n):
        pltpu.make_async_remote_copy(
            src_ref=x_ref.at[srcs[d]],
            dst_ref=recv.at[srcs[d]],
            send_sem=ssem1.at[d],
            recv_sem=rsem1.at[d],
            device_id=_device(axis, srcs[d]),
            device_id_type=MESH,
        ).wait_recv()
        acc = acc + recv[srcs[d]]
    gath[me] = acc

    sends2 = []
    for d in range(1, n):
        c = pltpu.make_async_remote_copy(
            src_ref=gath.at[me],
            dst_ref=gath.at[me],
            send_sem=ssem2.at[d],
            recv_sem=rsem2.at[d],
            device_id=_device(axis, peers[d]),
            device_id_type=MESH,
        )
        c.start()
        sends2.append(c)
    for c in sends:
        c.wait_send()
    for d in range(1, n):
        pltpu.make_async_remote_copy(
            src_ref=gath.at[srcs[d]],
            dst_ref=gath.at[srcs[d]],
            send_sem=ssem2.at[d],
            recv_sem=rsem2.at[d],
            device_id=_device(axis, srcs[d]),
            device_id_type=MESH,
        ).wait_recv()
    for c in sends2:
        c.wait_send()
    o_ref[...] = gath[...]


def allreduce(x, axis, n, cid):
    rows, width = x.shape
    chunk = rows // n
    xs = x.reshape(n, chunk, width)
    out = pl.pallas_call(
        functools.partial(_allreduce_kernel, axis, n),
        out_shape=jax.ShapeDtypeStruct(xs.shape, xs.dtype),
        in_specs=[pl.BlockSpec(memory_space=pltpu.VMEM)],
        out_specs=pl.BlockSpec(memory_space=pltpu.VMEM),
        scratch_shapes=[
            pltpu.VMEM(xs.shape, xs.dtype),
            pltpu.VMEM(xs.shape, xs.dtype),
            pltpu.SemaphoreType.DMA((n,)),
            pltpu.SemaphoreType.DMA((n,)),
            pltpu.SemaphoreType.DMA((n,)),
            pltpu.SemaphoreType.DMA((n,)),
        ],
        compiler_params=pltpu.CompilerParams(collective_id=cid, has_side_effects=True),
    )(xs)
    return out.reshape(rows, width)


def per_device(n_rows, n_feat, design, labels, local_x, dual_u, consensus_z, step_size, rho, penalty):
    x = local_x[0]
    dual = dual_u[0]
    sign = labels.astype(jnp.float32)
    eta = step_size[:, None]
    weight = rho[:, None]
    for turn in range(2):
        xb = x.astype(jnp.bfloat16)
        partial_margin = lax.dot_general(
            xb, design, (((1,), (1,)), ((), ())), preferred_element_type=jnp.float32
        )
        margin = allreduce(partial_margin, "feat", n_feat, 0)
        resid = (sign * jax.nn.sigmoid(-sign * margin)).astype(jnp.bfloat16)
        grad = jnp.dot(resid, design, preferred_element_type=jnp.float32)
        x = x - eta * (weight * (x - consensus_z + dual) - grad)
    limit = (penalty / (rho * n_rows))[:, None]
    total = allreduce(x + dual, "rows", n_rows, 1)
    mean = total / n_rows
    new_z = mean - jnp.clip(mean, -limit, limit)
    new_u = dual + x - new_z
    return (x[None], new_z, new_u[None])


def solution(mesh):
    in_specs = (
        P("rows", "feat"),
        P(None, "rows"),
        P("rows", None, "feat"),
        P("rows", None, "feat"),
        P(None, "feat"),
        P(),
        P(),
        P(),
    )
    out_specs = (P("rows", None, "feat"), P(None, "feat"), P("rows", None, "feat"))
    fn = functools.partial(per_device, mesh.shape["rows"], mesh.shape["feat"])
    return jax.shard_map(
        fn, mesh=mesh, in_specs=in_specs, out_specs=out_specs, check_vma=False
    )
```

```python
import functools

import jax
import jax.numpy as jnp
from jax import lax
from jax.experimental import pallas as pl
from jax.experimental.pallas import tpu as pltpu
from jax.sharding import PartitionSpec as P

MESH = pl.DeviceIdType.MESH
AXES = ("rows", "feat")


def _device(axis, peer):
    return tuple(peer if a == axis else lax.axis_index(a) for a in AXES)


def _allreduce_kernel(axis, n, rh, cw, x_ref, o_ref, recv, gath, ssem1, rsem1, ssem2, rsem2):
    me = lax.axis_index(axis)
    peers = [lax.rem(me + d, n) for d in range(n)]
    srcs = [lax.rem(me + n - d, n) for d in range(n)]
    cblocks = x_ref.shape[1] // cw

    def block(ref, p):
        r = pl.multiple_of((p // cblocks) * rh, 8)
        c = pl.multiple_of((p % cblocks) * cw, 128)
        return ref.at[pl.ds(r, rh), pl.ds(c, cw)]

    barrier = pltpu.get_barrier_semaphore()
    for d in range(1, n):
        pl.semaphore_signal(barrier, inc=1, device_id=_device(axis, peers[d]), device_id_type=MESH)
    pl.semaphore_wait(barrier, n - 1)

    sends = []
    for d in range(1, n):
        c = pltpu.make_async_remote_copy(
            src_ref=block(x_ref, peers[d]),
            dst_ref=recv.at[me],
            send_sem=ssem1.at[d],
            recv_sem=rsem1.at[d],
            device_id=_device(axis, peers[d]),
            device_id_type=MESH,
        )
        c.start()
        sends.append(c)
    acc = block(x_ref, me)[...]
    for d in range(1, n):
        pltpu.make_async_remote_copy(
            src_ref=recv.at[srcs[d]],
            dst_ref=recv.at[srcs[d]],
            send_sem=ssem1.at[d],
            recv_sem=rsem1.at[d],
            device_id=_device(axis, srcs[d]),
            device_id_type=MESH,
        ).wait_recv()
        acc = acc + recv[srcs[d]]
    gath[me] = acc

    sends2 = []
    for d in range(1, n):
        c = pltpu.make_async_remote_copy(
            src_ref=gath.at[me],
            dst_ref=gath.at[me],
            send_sem=ssem2.at[d],
            recv_sem=rsem2.at[d],
            device_id=_device(axis, peers[d]),
            device_id_type=MESH,
        )
        c.start()
        sends2.append(c)
    for c in sends:
        c.wait_send()
    for d in range(1, n):
        pltpu.make_async_remote_copy(
            src_ref=gath.at[srcs[d]],
            dst_ref=gath.at[srcs[d]],
            send_sem=ssem2.at[d],
            recv_sem=rsem2.at[d],
            device_id=_device(axis, srcs[d]),
            device_id_type=MESH,
        ).wait_recv()
    for c in sends2:
        c.wait_send()
    for p in range(n):
        r, c = (p // cblocks) * rh, (p % cblocks) * cw
        o_ref[r:r + rh, c:c + cw] = gath[p]


def allreduce(x, axis, n, cid):
    rows, width = x.shape
    rblocks = min(rows // 8, n)
    rh, cw = rows // rblocks, width * rblocks // n
    return pl.pallas_call(
        functools.partial(_allreduce_kernel, axis, n, rh, cw),
        out_shape=jax.ShapeDtypeStruct(x.shape, x.dtype),
        in_specs=[pl.BlockSpec(memory_space=pltpu.VMEM)],
        out_specs=pl.BlockSpec(memory_space=pltpu.VMEM),
        scratch_shapes=[
            pltpu.VMEM((n, rh, cw), x.dtype),
            pltpu.VMEM((n, rh, cw), x.dtype),
            pltpu.SemaphoreType.DMA((n,)),
            pltpu.SemaphoreType.DMA((n,)),
            pltpu.SemaphoreType.DMA((n,)),
            pltpu.SemaphoreType.DMA((n,)),
        ],
        compiler_params=pltpu.CompilerParams(collective_id=cid, has_side_effects=True),
    )(x)


def per_device(n_rows, n_feat, design, labels, local_x, dual_u, consensus_z, step_size, rho, penalty):
    x = local_x[0]
    dual = dual_u[0]
    sign = labels.astype(jnp.float32)
    eta = step_size[:, None]
    weight = rho[:, None]
    for turn in range(2):
        xb = x.astype(jnp.bfloat16)
        partial_margin = lax.dot_general(
            xb, design, (((1,), (1,)), ((), ())), preferred_element_type=jnp.float32
        )
        margin = allreduce(partial_margin, "feat", n_feat, 0)
        resid = (sign * jax.nn.sigmoid(-sign * margin)).astype(jnp.bfloat16)
        grad = jnp.dot(resid, design, preferred_element_type=jnp.float32)
        x = x - eta * (weight * (x - consensus_z + dual) - grad)
    limit = (penalty / (rho * n_rows))[:, None]
    total = allreduce(x + dual, "rows", n_rows, 1)
    mean = total / n_rows
    new_z = mean - jnp.clip(mean, -limit, limit)
    new_u = dual + x - new_z
    return (x[None], new_z, new_u[None])


def solution(mesh):
    in_specs = (
        P("rows", "feat"),
        P(None, "rows"),
        P("rows", None, "feat"),
        P("rows", None, "feat"),
        P(None, "feat"),
        P(),
        P(),
        P(),
    )
    out_specs = (P("rows", None, "feat"), P(None, "feat"), P("rows", None, "feat"))
    fn = functools.partial(per_device, mesh.shape["rows"], mesh.shape["feat"])
    return jax.shard_map(
        fn, mesh=mesh, in_specs=in_specs, out_specs=out_specs, check_vma=False
    )
```

```python
import functools

import jax
import jax.numpy as jnp
from jax import lax
from jax.experimental import pallas as pl
from jax.experimental.pallas import tpu as pltpu
from jax.sharding import PartitionSpec as P

MESH = pl.DeviceIdType.MESH
AXES = ("rows", "feat")


def _device(axis, peer):
    return tuple(peer if a == axis else lax.axis_index(a) for a in AXES)


def _allreduce_kernel(axis, n, rh, cw, x_ref, o_ref, recv, gath, ssem1, rsem1, ssem2, rsem2):
    me = lax.axis_index(axis)
    peers = [lax.rem(me + d, n) for d in range(n)]
    srcs = [lax.rem(me + n - d, n) for d in range(n)]
    cblocks = x_ref.shape[1] // cw

    def block(ref, p):
        r = pl.multiple_of((p // cblocks) * rh, 8)
        c = pl.multiple_of((p % cblocks) * cw, 128)
        return ref.at[pl.ds(r, rh), pl.ds(c, cw)]

    barrier = pltpu.get_barrier_semaphore()
    for d in range(1, n):
        pl.semaphore_signal(barrier, inc=1, device_id=_device(axis, peers[d]), device_id_type=MESH)
    pl.semaphore_wait(barrier, n - 1)

    sends = []
    for d in range(1, n):
        c = pltpu.make_async_remote_copy(
            src_ref=block(x_ref, peers[d]),
            dst_ref=recv.at[me],
            send_sem=ssem1.at[d],
            recv_sem=rsem1.at[d],
            device_id=_device(axis, peers[d]),
            device_id_type=MESH,
        )
        c.start()
        sends.append(c)
    acc = block(x_ref, me)[...]
    for d in range(1, n):
        pltpu.make_async_remote_copy(
            src_ref=recv.at[srcs[d]],
            dst_ref=recv.at[srcs[d]],
            send_sem=ssem1.at[d],
            recv_sem=rsem1.at[d],
            device_id=_device(axis, srcs[d]),
            device_id_type=MESH,
        ).wait_recv()
        acc = acc + recv[srcs[d]]
    gath[me] = acc

    sends2 = []
    for d in range(1, n):
        c = pltpu.make_async_remote_copy(
            src_ref=gath.at[me],
            dst_ref=gath.at[me],
            send_sem=ssem2.at[d],
            recv_sem=rsem2.at[d],
            device_id=_device(axis, peers[d]),
            device_id_type=MESH,
        )
        c.start()
        sends2.append(c)
    for c in sends:
        c.wait_send()
    for d in range(1, n):
        pltpu.make_async_remote_copy(
            src_ref=gath.at[srcs[d]],
            dst_ref=gath.at[srcs[d]],
            send_sem=ssem2.at[d],
            recv_sem=rsem2.at[d],
            device_id=_device(axis, srcs[d]),
            device_id_type=MESH,
        ).wait_recv()
    for c in sends2:
        c.wait_send()
    for p in range(n):
        r, c = (p // cblocks) * rh, (p % cblocks) * cw
        o_ref[r:r + rh, c:c + cw] = gath[p]


def allreduce(x, axis, n, cid):
    if n == 1:
        return x
    rows, width = x.shape
    rblocks = min(rows // 8, n)
    rh, cw = rows // rblocks, width * rblocks // n
    return pl.pallas_call(
        functools.partial(_allreduce_kernel, axis, n, rh, cw),
        out_shape=jax.ShapeDtypeStruct(x.shape, x.dtype),
        in_specs=[pl.BlockSpec(memory_space=pltpu.VMEM)],
        out_specs=pl.BlockSpec(memory_space=pltpu.VMEM),
        scratch_shapes=[
            pltpu.VMEM((n, rh, cw), x.dtype),
            pltpu.VMEM((n, rh, cw), x.dtype),
            pltpu.SemaphoreType.DMA((n,)),
            pltpu.SemaphoreType.DMA((n,)),
            pltpu.SemaphoreType.DMA((n,)),
            pltpu.SemaphoreType.DMA((n,)),
        ],
        compiler_params=pltpu.CompilerParams(collective_id=cid, has_side_effects=True),
    )(x)


def _rows_kernel(nx, x_ref, o_ref, ra, hbuf, rb, rc, gb, ge,
                 ssa, rsa, ssb, rsb, ssc, rsc, ssd, rsd, sse, rse):
    r = lax.axis_index("rows")
    n = 4 * nx
    half, blk = x_ref.shape[0] // 2, x_ref.shape[0] // (2 * nx)
    c = lax.rem(r, 2)
    xi = lax.rem(r // 2, nx)
    base = r - 2 * xi
    partner = r + 1 - 2 * c
    xpeers = [base + 2 * lax.rem(xi + d, nx) for d in range(nx)]
    xsrcs = [lax.rem(xi + nx - d, nx) for d in range(nx)]
    zpeer = lax.rem(r + 2 * nx, n)

    def dev(p):
        return _device("rows", p)

    def rcopy(src, dst, ss, rs, p):
        return pltpu.make_async_remote_copy(
            src_ref=src, dst_ref=dst, send_sem=ss, recv_sem=rs,
            device_id=dev(p), device_id_type=MESH)

    barrier = pltpu.get_barrier_semaphore()
    for p in [partner, zpeer] + xpeers[1:]:
        pl.semaphore_signal(barrier, inc=1, device_id=dev(p), device_id_type=MESH)
    pl.semaphore_wait(barrier, nx + 1)

    mine = pl.multiple_of(c * half, 8)
    other = pl.multiple_of((1 - c) * half, 8)
    a = rcopy(x_ref.at[pl.ds(other, half)], ra, ssa, rsa, partner)
    a.start()
    a.wait()
    hbuf[...] = x_ref[pl.ds(mine, half), :] + ra[...]

    bs = []
    for d in range(1, nx):
        j = lax.rem(xi + d, nx)
        cp = rcopy(hbuf.at[pl.ds(pl.multiple_of(j * blk, 8), blk)], rb.at[xi],
                   ssb.at[d], rsb.at[d], xpeers[d])
        cp.start()
        bs.append(cp)
    acc = hbuf[pl.ds(pl.multiple_of(xi * blk, 8), blk), :]
    for d in range(1, nx):
        rcopy(rb.at[xsrcs[d]], rb.at[xsrcs[d]], ssb.at[d], rsb.at[d], xpeers[d]).wait_recv()
        acc = acc + rb[xsrcs[d]]
    gb[xi] = acc

    cz = rcopy(gb.at[xi], rc, ssc, rsc, zpeer)
    cz.start()
    cz.wait()
    gb[xi] = gb[xi] + rc[...]

    ds_ = []
    for d in range(1, nx):
        cp = rcopy(gb.at[xi], gb.at[xi], ssd.at[d], rsd.at[d], xpeers[d])
        cp.start()
        ds_.append(cp)
    for cp in bs:
        cp.wait_send()
    for d in range(1, nx):
        rcopy(gb.at[xsrcs[d]], gb.at[xsrcs[d]], ssd.at[d], rsd.at[d], xpeers[d]).wait_recv()
    for cp in ds_:
        cp.wait_send()

    e = rcopy(gb, ge, sse, rse, partner)
    e.start()
    e.wait()
    for j in range(nx):
        o_ref[pl.ds(pl.multiple_of(mine + j * blk, 8), blk), :] = gb[j]
        o_ref[pl.ds(pl.multiple_of(other + j * blk, 8), blk), :] = ge[j]


def rows_allreduce(x, n, cid):
    rows, width = x.shape
    nx = n // 4
    half, blk = rows // 2, rows // (2 * nx)
    dma = pltpu.SemaphoreType.DMA
    return pl.pallas_call(
        functools.partial(_rows_kernel, nx),
        out_shape=jax.ShapeDtypeStruct(x.shape, x.dtype),
        in_specs=[pl.BlockSpec(memory_space=pltpu.VMEM)],
        out_specs=pl.BlockSpec(memory_space=pltpu.VMEM),
        scratch_shapes=[
            pltpu.VMEM((half, width), x.dtype),
            pltpu.VMEM((half, width), x.dtype),
            pltpu.VMEM((nx, blk, width), x.dtype),
            pltpu.VMEM((blk, width), x.dtype),
            pltpu.VMEM((nx, blk, width), x.dtype),
            pltpu.VMEM((nx, blk, width), x.dtype),
            dma(()), dma(()), dma((nx,)), dma((nx,)), dma(()), dma(()),
            dma((nx,)), dma((nx,)), dma(()), dma(()),
        ],
        compiler_params=pltpu.CompilerParams(collective_id=cid, has_side_effects=True),
    )(x)


def per_device(n_rows, n_feat, design, labels, local_x, dual_u, consensus_z, step_size, rho, penalty):
    x = local_x[0]
    dual = dual_u[0]
    sign = labels.astype(jnp.float32)
    eta = step_size[:, None]
    weight = rho[:, None]
    for turn in range(2):
        xb = x.astype(jnp.bfloat16)
        partial_margin = lax.dot_general(
            xb, design, (((1,), (1,)), ((), ())), preferred_element_type=jnp.float32
        )
        margin = allreduce(partial_margin, "feat", n_feat, 0)
        resid = (sign * jax.nn.sigmoid(-sign * margin)).astype(jnp.bfloat16)
        grad = jnp.dot(resid, design, preferred_element_type=jnp.float32)
        x = x - eta * (weight * (x - consensus_z + dual) - grad)
    limit = (penalty / (rho * n_rows))[:, None]
    total = rows_allreduce(x + dual, n_rows, 1)
    mean = total / n_rows
    new_z = mean - jnp.clip(mean, -limit, limit)
    new_u = dual + x - new_z
    return (x[None], new_z, new_u[None])


def solution(mesh):
    in_specs = (
        P("rows", "feat"),
        P(None, "rows"),
        P("rows", None, "feat"),
        P("rows", None, "feat"),
        P(None, "feat"),
        P(),
        P(),
        P(),
    )
    out_specs = (P("rows", None, "feat"), P(None, "feat"), P("rows", None, "feat"))
    fn = functools.partial(per_device, mesh.shape["rows"], mesh.shape["feat"])
    return jax.shard_map(
        fn, mesh=mesh, in_specs=in_specs, out_specs=out_specs, check_vma=False
    )
```

```python
import functools

import jax
import jax.numpy as jnp
from jax import lax
from jax.experimental import pallas as pl
from jax.experimental.pallas import tpu as pltpu
from jax.sharding import PartitionSpec as P

MESH = pl.DeviceIdType.MESH
AXES = ("rows", "feat")
TILE = 512


def _device(axis, peer):
    return tuple(peer if a == axis else lax.axis_index(a) for a in AXES)


def _rcopy(axis, src, dst, ss, rs, p):
    return pltpu.make_async_remote_copy(
        src_ref=src, dst_ref=dst, send_sem=ss, recv_sem=rs,
        device_id=_device(axis, p), device_id_type=MESH)


def _feat_allreduce(n, rh, cw, x_ref, o_ref, recv, gath, ss1, rs1, ss2, rs2):
    me = lax.axis_index("feat")
    peers = [lax.rem(me + d, n) for d in range(n)]
    srcs = [lax.rem(me + n - d, n) for d in range(n)]
    cblocks = x_ref.shape[1] // cw

    def block(ref, p):
        r = pl.multiple_of((p // cblocks) * rh, 8)
        c = pl.multiple_of((p % cblocks) * cw, 128)
        return ref.at[pl.ds(r, rh), pl.ds(c, cw)]

    sends = []
    for d in range(1, n):
        c = _rcopy("feat", block(x_ref, peers[d]), recv.at[me], ss1.at[d], rs1.at[d], peers[d])
        c.start()
        sends.append(c)
    acc = block(x_ref, me)[...]
    for d in range(1, n):
        _rcopy("feat", recv.at[srcs[d]], recv.at[srcs[d]], ss1.at[d], rs1.at[d], srcs[d]).wait_recv()
        acc = acc + recv[srcs[d]]
    gath[me] = acc
    sends2 = []
    for d in range(1, n):
        c = _rcopy("feat", gath.at[me], gath.at[me], ss2.at[d], rs2.at[d], peers[d])
        c.start()
        sends2.append(c)
    for c in sends:
        c.wait_send()
    for d in range(1, n):
        _rcopy("feat", gath.at[srcs[d]], gath.at[srcs[d]], ss2.at[d], rs2.at[d], srcs[d]).wait_recv()
    for c in sends2:
        c.wait_send()
    for p in range(n):
        r, c = (p // cblocks) * rh, (p % cblocks) * cw
        o_ref[r:r + rh, c:c + cw] = gath[p]


def _rows_allreduce(nx, x_ref, o_ref, ra, hbuf, rb, rc, gb, ge,
                    ssa, rsa, ssb, rsb, ssc, rsc, ssd, rsd, sse, rse):
    r = lax.axis_index("rows")
    n = 4 * nx
    half, blk = x_ref.shape[0] // 2, x_ref.shape[0] // (2 * nx)
    c = lax.rem(r, 2)
    xi = lax.rem(r // 2, nx)
    base = r - 2 * xi
    partner = r + 1 - 2 * c
    xpeers = [base + 2 * lax.rem(xi + d, nx) for d in range(nx)]
    xsrcs = [lax.rem(xi + nx - d, nx) for d in range(nx)]
    zpeer = lax.rem(r + 2 * nx, n)
    rcopy = functools.partial(_rcopy, "rows")

    mine = pl.multiple_of(c * half, 8)
    other = pl.multiple_of((1 - c) * half, 8)
    a = rcopy(x_ref.at[pl.ds(other, half)], ra, ssa, rsa, partner)
    a.start()
    a.wait()
    hbuf[...] = x_ref[pl.ds(mine, half), :] + ra[...]

    bs = []
    for d in range(1, nx):
        j = lax.rem(xi + d, nx)
        cp = rcopy(hbuf.at[pl.ds(pl.multiple_of(j * blk, 8), blk)], rb.at[xi],
                   ssb.at[d], rsb.at[d], xpeers[d])
        cp.start()
        bs.append(cp)
    acc = hbuf[pl.ds(pl.multiple_of(xi * blk, 8), blk), :]
    for d in range(1, nx):
        rcopy(rb.at[xsrcs[d]], rb.at[xsrcs[d]], ssb.at[d], rsb.at[d], xpeers[d]).wait_recv()
        acc = acc + rb[xsrcs[d]]
    gb[xi] = acc

    cz = rcopy(gb.at[xi], rc, ssc, rsc, zpeer)
    cz.start()
    cz.wait()
    gb[xi] = gb[xi] + rc[...]

    ds_ = []
    for d in range(1, nx):
        cp = rcopy(gb.at[xi], gb.at[xi], ssd.at[d], rsd.at[d], xpeers[d])
        cp.start()
        ds_.append(cp)
    for cp in bs:
        cp.wait_send()
    for d in range(1, nx):
        rcopy(gb.at[xsrcs[d]], gb.at[xsrcs[d]], ssd.at[d], rsd.at[d], xpeers[d]).wait_recv()
    for cp in ds_:
        cp.wait_send()

    e = rcopy(gb, ge, sse, rse, partner)
    e.start()
    e.wait()
    for j in range(nx):
        o_ref[pl.ds(pl.multiple_of(mine + j * blk, 8), blk), :] = gb[j]
        o_ref[pl.ds(pl.multiple_of(other + j * blk, 8), blk), :] = ge[j]


def _fused_kernel(nf, nr, rh, cw, design, lab, x0, dual, cz, eta, rho, lim,
                  ox, oz, ou, pbuf, mbuf, rbuf, sbuf, *scratch):
    feat_scr = scratch[:12]
    rows_scr = scratch[12:]
    nx = nr // 4

    me_f = lax.axis_index("feat")
    r = lax.axis_index("rows")
    fpeers = [lax.rem(me_f + d, nf) for d in range(1, nf)]
    c = lax.rem(r, 2)
    xi = lax.rem(r // 2, nx)
    rpeers = [r + 1 - 2 * c, lax.rem(r + 2 * nx, nr)]
    rpeers += [r - 2 * xi + 2 * lax.rem(xi + d, nx) for d in range(1, nx)]

    barrier = pltpu.get_barrier_semaphore()
    for p in fpeers:
        pl.semaphore_signal(barrier, inc=1, device_id=_device("feat", p), device_id_type=MESH)
    for p in rpeers:
        pl.semaphore_signal(barrier, inc=1, device_id=_device("rows", p), device_id_type=MESH)
    pl.semaphore_wait(barrier, len(fpeers) + len(rpeers))

    ox[...] = x0[...]
    ntile = design.shape[1] // TILE
    for turn in range(2):
        def margin_body(k, acc):
            cols = pl.ds(pl.multiple_of(k * TILE, TILE), TILE)
            xk = ox[:, cols].astype(jnp.bfloat16)
            return acc + lax.dot_general(
                xk, design[:, cols], (((1,), (1,)), ((), ())),
                preferred_element_type=jnp.float32)

        pbuf[...] = lax.fori_loop(0, ntile, margin_body, jnp.zeros(pbuf.shape, jnp.float32))
        _feat_allreduce(nf, rh, cw, pbuf, mbuf, *feat_scr[turn * 6:(turn + 1) * 6])
        sign = lab[...].astype(jnp.float32)
        rbuf[...] = (sign * jax.nn.sigmoid(-sign * mbuf[...])).astype(jnp.bfloat16)

        def grad_body(j, carry):
            cols = pl.ds(pl.multiple_of(j * TILE, TILE), TILE)
            g = jnp.dot(rbuf[...], design[:, cols], preferred_element_type=jnp.float32)
            x = ox[:, cols]
            ox[:, cols] = x - eta[...] * (rho[...] * (x - cz[:, cols] + dual[:, cols]) - g)
            return carry

        lax.fori_loop(0, ntile, grad_body, 0)

    sbuf[...] = ox[...] + dual[...]
    _rows_allreduce(nx, sbuf, oz, *rows_scr)
    mean = oz[...] / nr
    new_z = mean - jnp.clip(mean, -lim[...], lim[...])
    oz[...] = new_z
    ou[...] = dual[...] + ox[...] - new_z


def _fused(n_rows, n_feat, design, labels, x0, dual, cz, eta, rho, lim):
    k, width = x0.shape
    s = design.shape[0]
    rblocks = min(k // 8, n_feat)
    rh, cw = k // rblocks, s * rblocks // n_feat
    nx = n_rows // 4
    half, blk = k // 2, k // (2 * nx)
    f32 = jnp.float32
    dma = pltpu.SemaphoreType.DMA
    feat_scr = []
    for _ in range(2):
        feat_scr += [pltpu.VMEM((n_feat, rh, cw), f32), pltpu.VMEM((n_feat, rh, cw), f32)]
        feat_scr += [dma((n_feat,)) for _ in range(4)]
    rows_scr = [
        pltpu.VMEM((half, width), f32),
        pltpu.VMEM((half, width), f32),
        pltpu.VMEM((nx, blk, width), f32),
        pltpu.VMEM((blk, width), f32),
        pltpu.VMEM((nx, blk, width), f32),
        pltpu.VMEM((nx, blk, width), f32),
        dma(()), dma(()), dma((nx,)), dma((nx,)), dma(()), dma(()),
        dma((nx,)), dma((nx,)), dma(()), dma(()),
    ]
    vmem = pl.BlockSpec(memory_space=pltpu.VMEM)
    out = jax.ShapeDtypeStruct((k, width), f32)
    return pl.pallas_call(
        functools.partial(_fused_kernel, n_feat, n_rows, rh, cw),
        out_shape=(out, out, out),
        in_specs=[vmem] * 8,
        out_specs=(vmem, vmem, vmem),
        scratch_shapes=[
            pltpu.VMEM((k, s), f32),
            pltpu.VMEM((k, s), f32),
            pltpu.VMEM((k, s), jnp.bfloat16),
            pltpu.VMEM((k, width), f32),
        ] + feat_scr + rows_scr,
        compiler_params=pltpu.CompilerParams(
            collective_id=0, has_side_effects=True, vmem_limit_bytes=60 * 1024 * 1024),
    )(design, labels, x0, dual, cz, eta, rho, lim)


def per_device(n_rows, n_feat, design, labels, local_x, dual_u, consensus_z, step_size, rho, penalty):
    eta = step_size[:, None]
    weight = rho[:, None]
    limit = (penalty / (rho * n_rows))[:, None]
    x, new_z, new_u = _fused(n_rows, n_feat, design, labels, local_x[0], dual_u[0],
                             consensus_z, eta, weight, limit)
    return (x[None], new_z, new_u[None])


def solution(mesh):
    in_specs = (
        P("rows", "feat"),
        P(None, "rows"),
        P("rows", None, "feat"),
        P("rows", None, "feat"),
        P(None, "feat"),
        P(),
        P(),
        P(),
    )
    out_specs = (P("rows", None, "feat"), P(None, "feat"), P("rows", None, "feat"))
    fn = functools.partial(per_device, mesh.shape["rows"], mesh.shape["feat"])
    return jax.shard_map(
        fn, mesh=mesh, in_specs=in_specs, out_specs=out_specs, check_vma=False
    )
```

```python
import functools

import jax
import jax.numpy as jnp
from jax import lax
from jax.experimental import pallas as pl
from jax.experimental.pallas import tpu as pltpu
from jax.sharding import PartitionSpec as P

MESH = pl.DeviceIdType.MESH
AXES = ("rows", "feat")
TILE = 512


def _device(axis, peer):
    return tuple(peer if a == axis else lax.axis_index(a) for a in AXES)


def _rcopy(axis, src, dst, ss, rs, p):
    return pltpu.make_async_remote_copy(
        src_ref=src, dst_ref=dst, send_sem=ss, recv_sem=rs,
        device_id=_device(axis, p), device_id_type=MESH)


def _feat_allreduce(n, rh, cw, x_ref, o_ref, recv, gath, ss1, rs1, ss2, rs2):
    me = lax.axis_index("feat")
    peers = [lax.rem(me + d, n) for d in range(n)]
    srcs = [lax.rem(me + n - d, n) for d in range(n)]
    cblocks = x_ref.shape[1] // cw

    def block(ref, p):
        r = pl.multiple_of((p // cblocks) * rh, 8)
        c = pl.multiple_of((p % cblocks) * cw, 128)
        return ref.at[pl.ds(r, rh), pl.ds(c, cw)]

    sends = []
    for d in range(1, n):
        c = _rcopy("feat", block(x_ref, peers[d]), recv.at[me], ss1.at[d], rs1.at[d], peers[d])
        c.start()
        sends.append(c)
    acc = block(x_ref, me)[...]
    for d in range(1, n):
        _rcopy("feat", recv.at[srcs[d]], recv.at[srcs[d]], ss1.at[d], rs1.at[d], srcs[d]).wait_recv()
        acc = acc + recv[srcs[d]]
    gath[me] = acc
    sends2 = []
    for d in range(1, n):
        c = _rcopy("feat", gath.at[me], gath.at[me], ss2.at[d], rs2.at[d], peers[d])
        c.start()
        sends2.append(c)
    for c in sends:
        c.wait_send()
    for d in range(1, n):
        _rcopy("feat", gath.at[srcs[d]], gath.at[srcs[d]], ss2.at[d], rs2.at[d], srcs[d]).wait_recv()
    for c in sends2:
        c.wait_send()
    for p in range(n):
        r, c = (p // cblocks) * rh, (p % cblocks) * cw
        o_ref[r:r + rh, c:c + cw] = gath[p]


def _rows_allreduce(nx, x_ref, o_ref, ra, hbuf, rb, rc, gb, ge,
                    ssa, rsa, ssb, rsb, ssc, rsc, ssd, rsd, sse, rse):
    r = lax.axis_index("rows")
    n = 4 * nx
    half, blk = x_ref.shape[0] // 2, x_ref.shape[0] // (2 * nx)
    c = lax.rem(r, 2)
    xi = lax.rem(r // 2, nx)
    base = r - 2 * xi
    partner = r + 1 - 2 * c
    xpeers = [base + 2 * lax.rem(xi + d, nx) for d in range(nx)]
    xsrcs = [lax.rem(xi + nx - d, nx) for d in range(nx)]
    zpeer = lax.rem(r + 2 * nx, n)
    rcopy = functools.partial(_rcopy, "rows")

    mine = pl.multiple_of(c * half, 8)
    other = pl.multiple_of((1 - c) * half, 8)
    a = rcopy(x_ref.at[pl.ds(other, half)], ra, ssa, rsa, partner)
    a.start()
    a.wait()
    hbuf[...] = x_ref[pl.ds(mine, half), :] + ra[...]

    bs = []
    for d in range(1, nx):
        j = lax.rem(xi + d, nx)
        cp = rcopy(hbuf.at[pl.ds(pl.multiple_of(j * blk, 8), blk)], rb.at[xi],
                   ssb.at[d], rsb.at[d], xpeers[d])
        cp.start()
        bs.append(cp)
    acc = hbuf[pl.ds(pl.multiple_of(xi * blk, 8), blk), :]
    for d in range(1, nx):
        rcopy(rb.at[xsrcs[d]], rb.at[xsrcs[d]], ssb.at[d], rsb.at[d], xpeers[d]).wait_recv()
        acc = acc + rb[xsrcs[d]]
    gb[xi] = acc

    cz = rcopy(gb.at[xi], rc, ssc, rsc, zpeer)
    cz.start()
    cz.wait()
    gb[xi] = gb[xi] + rc[...]

    ds_ = []
    for d in range(1, nx):
        cp = rcopy(gb.at[xi], gb.at[xi], ssd.at[d], rsd.at[d], xpeers[d])
        cp.start()
        ds_.append(cp)
    for cp in bs:
        cp.wait_send()
    for d in range(1, nx):
        rcopy(gb.at[xsrcs[d]], gb.at[xsrcs[d]], ssd.at[d], rsd.at[d], xpeers[d]).wait_recv()
    for cp in ds_:
        cp.wait_send()

    e = rcopy(gb, ge, sse, rse, partner)
    e.start()
    e.wait()
    for j in range(nx):
        o_ref[pl.ds(pl.multiple_of(mine + j * blk, 8), blk), :] = gb[j]
        o_ref[pl.ds(pl.multiple_of(other + j * blk, 8), blk), :] = ge[j]


def _fused_kernel(nf, nr, rh, cw, design, lab, x0, dual, cz, prm,
                  ox, ot, pbuf, mbuf, rbuf, sbuf, *scratch):
    feat_scr = scratch[:12]
    rows_scr = scratch[12:]
    nx = nr // 4

    me_f = lax.axis_index("feat")
    r = lax.axis_index("rows")
    fpeers = [lax.rem(me_f + d, nf) for d in range(1, nf)]
    c = lax.rem(r, 2)
    xi = lax.rem(r // 2, nx)
    rpeers = [r + 1 - 2 * c, lax.rem(r + 2 * nx, nr)]
    rpeers += [r - 2 * xi + 2 * lax.rem(xi + d, nx) for d in range(1, nx)]

    barrier = pltpu.get_barrier_semaphore()
    for p in fpeers:
        pl.semaphore_signal(barrier, inc=1, device_id=_device("feat", p), device_id_type=MESH)
    for p in rpeers:
        pl.semaphore_signal(barrier, inc=1, device_id=_device("rows", p), device_id_type=MESH)
    pl.semaphore_wait(barrier, len(fpeers) + len(rpeers))

    eta = prm[:, 0:1]
    rho = prm[:, 1:2]
    ox[...] = x0[...]
    ntile = design.shape[1] // TILE
    for turn in range(2):
        def margin_body(k, acc):
            cols = pl.ds(pl.multiple_of(k * TILE, TILE), TILE)
            xk = ox[:, cols].astype(jnp.bfloat16)
            return acc + lax.dot_general(
                xk, design[:, cols], (((1,), (1,)), ((), ())),
                preferred_element_type=jnp.float32)

        pbuf[...] = lax.fori_loop(0, ntile, margin_body, jnp.zeros(pbuf.shape, jnp.float32))
        _feat_allreduce(nf, rh, cw, pbuf, mbuf, *feat_scr[turn * 6:(turn + 1) * 6])
        sign = lab[...].astype(jnp.float32)
        rbuf[...] = (sign * jax.nn.sigmoid(-sign * mbuf[...])).astype(jnp.bfloat16)

        def grad_body(j, carry):
            cols = pl.ds(pl.multiple_of(j * TILE, TILE), TILE)
            g = jnp.dot(rbuf[...], design[:, cols], preferred_element_type=jnp.float32)
            x = ox[:, cols]
            ox[:, cols] = x - eta * (rho * (x - cz[:, cols] + dual[:, cols]) - g)
            return carry

        lax.fori_loop(0, ntile, grad_body, 0)

    sbuf[...] = ox[...] + dual[...]
    _rows_allreduce(nx, sbuf, ot, *rows_scr)


def _final_kernel(nr, x, total, dual, prm, ox, oz, ou):
    lim = prm[:, 2:3]
    mean = total[...] / nr
    new_z = mean - jnp.clip(mean, -lim, lim)
    ox[...] = x[...]
    oz[...] = new_z
    ou[...] = dual[...] + x[...] - new_z


def _fused(n_rows, n_feat, design, labels, x0, dual, cz, prm):
    k, width = x0.shape
    s = design.shape[0]
    rblocks = min(k // 8, n_feat)
    rh, cw = k // rblocks, s * rblocks // n_feat
    nx = n_rows // 4
    half, blk = k // 2, k // (2 * nx)
    f32 = jnp.float32
    dma = pltpu.SemaphoreType.DMA
    feat_scr = []
    for _ in range(2):
        feat_scr += [pltpu.VMEM((n_feat, rh, cw), f32), pltpu.VMEM((n_feat, rh, cw), f32)]
        feat_scr += [dma((n_feat,)) for _ in range(4)]
    rows_scr = [
        pltpu.VMEM((half, width), f32),
        pltpu.VMEM((half, width), f32),
        pltpu.VMEM((nx, blk, width), f32),
        pltpu.VMEM((blk, width), f32),
        pltpu.VMEM((nx, blk, width), f32),
        pltpu.VMEM((nx, blk, width), f32),
        dma(()), dma(()), dma((nx,)), dma((nx,)), dma(()), dma(()),
        dma((nx,)), dma((nx,)), dma(()), dma(()),
    ]
    vmem = pl.BlockSpec(memory_space=pltpu.VMEM)
    out = jax.ShapeDtypeStruct((k, width), f32)
    x, total = pl.pallas_call(
        functools.partial(_fused_kernel, n_feat, n_rows, rh, cw),
        out_shape=(out, out),
        in_specs=[vmem] * 6,
        out_specs=(vmem, vmem),
        scratch_shapes=[
            pltpu.VMEM((k, s), f32),
            pltpu.VMEM((k, s), f32),
            pltpu.VMEM((k, s), jnp.bfloat16),
            pltpu.VMEM((k, width), f32),
        ] + feat_scr + rows_scr,
        compiler_params=pltpu.CompilerParams(
            collective_id=0, has_side_effects=True, vmem_limit_bytes=60 * 1024 * 1024),
    )(design, labels, x0, dual, cz, prm)
    return pl.pallas_call(
        functools.partial(_final_kernel, n_rows),
        out_shape=(out, out, out),
        in_specs=[vmem] * 4,
        out_specs=(vmem, vmem, vmem),
    )(x, total, dual, prm)


def per_device(n_rows, n_feat, design, labels, local_x, dual_u, consensus_z, step_size, rho, penalty):
    prm = jnp.stack([step_size, rho, penalty / (rho * n_rows)], axis=1)
    x, new_z, new_u = _fused(n_rows, n_feat, design, labels, local_x[0], dual_u[0],
                             consensus_z, prm)
    return (x[None], new_z, new_u[None])


def solution(mesh):
    in_specs = (
        P("rows", "feat"),
        P(None, "rows"),
        P("rows", None, "feat"),
        P("rows", None, "feat"),
        P(None, "feat"),
        P(),
        P(),
        P(),
    )
    out_specs = (P("rows", None, "feat"), P(None, "feat"), P("rows", None, "feat"))
    fn = functools.partial(per_device, mesh.shape["rows"], mesh.shape["feat"])
    return jax.shard_map(
        fn, mesh=mesh, in_specs=in_specs, out_specs=out_specs, check_vma=False
    )
```

```python
import functools

import jax
import jax.numpy as jnp
from jax import lax
from jax.experimental import pallas as pl
from jax.experimental.pallas import tpu as pltpu
from jax.sharding import PartitionSpec as P

MESH = pl.DeviceIdType.MESH
AXES = ("rows", "feat")
TILE = 512
QCH = 4


def _device(axis, peer):
    return tuple(peer if a == axis else lax.axis_index(a) for a in AXES)


def _rcopy(axis, src, dst, ss, rs, p):
    return pltpu.make_async_remote_copy(
        src_ref=src, dst_ref=dst, send_sem=ss, recv_sem=rs,
        device_id=_device(axis, p), device_id_type=MESH)


def _feat_allreduce(n, rh, cw, x_ref, o_ref, recv, gath, ss1, rs1, ss2, rs2):
    me = lax.axis_index("feat")
    peers = [lax.rem(me + d, n) for d in range(n)]
    srcs = [lax.rem(me + n - d, n) for d in range(n)]
    cblocks = x_ref.shape[1] // cw

    def block(ref, p):
        r = pl.multiple_of((p // cblocks) * rh, 8)
        c = pl.multiple_of((p % cblocks) * cw, 128)
        return ref.at[pl.ds(r, rh), pl.ds(c, cw)]

    sends = []
    for d in range(1, n):
        c = _rcopy("feat", block(x_ref, peers[d]), recv.at[me], ss1.at[d], rs1.at[d], peers[d])
        c.start()
        sends.append(c)
    acc = block(x_ref, me)[...]
    for d in range(1, n):
        _rcopy("feat", recv.at[srcs[d]], recv.at[srcs[d]], ss1.at[d], rs1.at[d], srcs[d]).wait_recv()
        acc = acc + recv[srcs[d]]
    gath[me] = acc
    sends2 = []
    for d in range(1, n):
        c = _rcopy("feat", gath.at[me], gath.at[me], ss2.at[d], rs2.at[d], peers[d])
        c.start()
        sends2.append(c)
    for c in sends:
        c.wait_send()
    for d in range(1, n):
        _rcopy("feat", gath.at[srcs[d]], gath.at[srcs[d]], ss2.at[d], rs2.at[d], srcs[d]).wait_recv()
    for c in sends2:
        c.wait_send()
    for p in range(n):
        r, c = (p // cblocks) * rh, (p % cblocks) * cw
        o_ref[r:r + rh, c:c + cw] = gath[p]


def _rows_allreduce(nx, x_ref, o_ref, ra, hbuf, rb, rc, gb, ge,
                    ssa, rsa, ssb, rsb, ssc, rsc, ssd, rsd, sse, rse):
    r = lax.axis_index("rows")
    n = 4 * nx
    half, blk = x_ref.shape[0] // 2, x_ref.shape[0] // (2 * nx)
    wq = x_ref.shape[1] // QCH
    c = lax.rem(r, 2)
    xi = lax.rem(r // 2, nx)
    base = r - 2 * xi
    partner = r + 1 - 2 * c
    xpeers = [base + 2 * lax.rem(xi + d, nx) for d in range(nx)]
    xsrcs = [lax.rem(xi + nx - d, nx) for d in range(nx)]
    zpeer = lax.rem(r + 2 * nx, n)
    rcopy = functools.partial(_rcopy, "rows")
    mine = pl.multiple_of(c * half, 8)
    other = pl.multiple_of((1 - c) * half, 8)

    def cols(q):
        return pl.ds(q * wq, wq)

    def rows_of(j):
        return pl.ds(pl.multiple_of(j * blk, 8), blk)

    a = []
    for q in range(QCH):
        cp = rcopy(x_ref.at[pl.ds(other, half), cols(q)], ra.at[:, cols(q)], ssa.at[q], rsa.at[q], partner)
        cp.start()
        a.append(cp)
    bs = []
    for q in range(QCH):
        a[q].wait()
        hbuf[:, cols(q)] = x_ref[pl.ds(mine, half), cols(q)] + ra[:, cols(q)]
        for d in range(1, nx):
            j = lax.rem(xi + d, nx)
            cp = rcopy(hbuf.at[rows_of(j), cols(q)], rb.at[xi, :, cols(q)],
                       ssb.at[q, d], rsb.at[q, d], xpeers[d])
            cp.start()
            bs.append(cp)
    cz = []
    for q in range(QCH):
        acc = hbuf[rows_of(xi), cols(q)]
        for d in range(1, nx):
            rcopy(rb.at[xsrcs[d], :, cols(q)], rb.at[xsrcs[d], :, cols(q)],
                  ssb.at[q, d], rsb.at[q, d], xpeers[d]).wait_recv()
            acc = acc + rb[xsrcs[d], :, cols(q)]
        gb[xi, :, cols(q)] = acc
        cp = rcopy(gb.at[xi, :, cols(q)], rc.at[:, cols(q)], ssc.at[q], rsc.at[q], zpeer)
        cp.start()
        cz.append(cp)
    ds_ = []
    for q in range(QCH):
        cz[q].wait()
        gb[xi, :, cols(q)] = gb[xi, :, cols(q)] + rc[:, cols(q)]
        for d in range(1, nx):
            cp = rcopy(gb.at[xi, :, cols(q)], gb.at[xi, :, cols(q)], ssd.at[q, d], rsd.at[q, d], xpeers[d])
            cp.start()
            ds_.append(cp)
    e = []
    for q in range(QCH):
        for d in range(1, nx):
            rcopy(gb.at[xsrcs[d], :, cols(q)], gb.at[xsrcs[d], :, cols(q)],
                  ssd.at[q, d], rsd.at[q, d], xpeers[d]).wait_recv()
        cp = rcopy(gb.at[:, :, cols(q)], ge.at[:, :, cols(q)], sse.at[q], rse.at[q], partner)
        cp.start()
        e.append(cp)
    for cp in bs + ds_:
        cp.wait_send()
    for q in range(QCH):
        e[q].wait()
        for j in range(nx):
            o_ref[pl.ds(pl.multiple_of(mine + j * blk, 8), blk), cols(q)] = gb[j, :, cols(q)]
            o_ref[pl.ds(pl.multiple_of(other + j * blk, 8), blk), cols(q)] = ge[j, :, cols(q)]


def _fused_kernel(nf, nr, rh, cw, design, lab, x0, dual, cz, prm,
                  ox, ot, pbuf, mbuf, rbuf, sbuf, *scratch):
    feat_scr = scratch[:12]
    rows_scr = scratch[12:]
    nx = nr // 4

    me_f = lax.axis_index("feat")
    r = lax.axis_index("rows")
    fpeers = [lax.rem(me_f + d, nf) for d in range(1, nf)]
    c = lax.rem(r, 2)
    xi = lax.rem(r // 2, nx)
    rpeers = [r + 1 - 2 * c, lax.rem(r + 2 * nx, nr)]
    rpeers += [r - 2 * xi + 2 * lax.rem(xi + d, nx) for d in range(1, nx)]

    barrier = pltpu.get_barrier_semaphore()
    for p in fpeers:
        pl.semaphore_signal(barrier, inc=1, device_id=_device("feat", p), device_id_type=MESH)
    for p in rpeers:
        pl.semaphore_signal(barrier, inc=1, device_id=_device("rows", p), device_id_type=MESH)
    pl.semaphore_wait(barrier, len(fpeers) + len(rpeers))

    eta = prm[:, 0:1]
    rho = prm[:, 1:2]
    ox[...] = x0[...]
    ntile = design.shape[1] // TILE
    for turn in range(2):
        def margin_body(k, acc):
            cols = pl.ds(pl.multiple_of(k * TILE, TILE), TILE)
            xk = ox[:, cols].astype(jnp.bfloat16)
            return acc + lax.dot_general(
                xk, design[:, cols], (((1,), (1,)), ((), ())),
                preferred_element_type=jnp.float32)

        pbuf[...] = lax.fori_loop(0, ntile, margin_body, jnp.zeros(pbuf.shape, jnp.float32))
        _feat_allreduce(nf, rh, cw, pbuf, mbuf, *feat_scr[turn * 6:(turn + 1) * 6])
        sign = lab[...].astype(jnp.float32)
        rbuf[...] = (sign * jax.nn.sigmoid(-sign * mbuf[...])).astype(jnp.bfloat16)

        def grad_body(j, carry):
            cols = pl.ds(pl.multiple_of(j * TILE, TILE), TILE)
            g = jnp.dot(rbuf[...], design[:, cols], preferred_element_type=jnp.float32)
            x = ox[:, cols]
            ox[:, cols] = x - eta * (rho * (x - cz[:, cols] + dual[:, cols]) - g)
            return carry

        lax.fori_loop(0, ntile, grad_body, 0)

    sbuf[...] = ox[...] + dual[...]
    _rows_allreduce(nx, sbuf, ot, *rows_scr)


def _final_kernel(nr, x, total, dual, prm, ox, oz, ou):
    lim = prm[:, 2:3]
    mean = total[...] / nr
    new_z = mean - jnp.clip(mean, -lim, lim)
    ox[...] = x[...]
    oz[...] = new_z
    ou[...] = dual[...] + x[...] - new_z


def _fused(n_rows, n_feat, design, labels, x0, dual, cz, prm):
    k, width = x0.shape
    s = design.shape[0]
    rblocks = min(k // 8, n_feat)
    rh, cw = k // rblocks, s * rblocks // n_feat
    nx = n_rows // 4
    half, blk = k // 2, k // (2 * nx)
    f32 = jnp.float32
    dma = pltpu.SemaphoreType.DMA
    feat_scr = []
    for _ in range(2):
        feat_scr += [pltpu.VMEM((n_feat, rh, cw), f32), pltpu.VMEM((n_feat, rh, cw), f32)]
        feat_scr += [dma((n_feat,)) for _ in range(4)]
    rows_scr = [
        pltpu.VMEM((half, width), f32),
        pltpu.VMEM((half, width), f32),
        pltpu.VMEM((nx, blk, width), f32),
        pltpu.VMEM((blk, width), f32),
        pltpu.VMEM((nx, blk, width), f32),
        pltpu.VMEM((nx, blk, width), f32),
        dma((QCH,)), dma((QCH,)), dma((QCH, nx)), dma((QCH, nx)), dma((QCH,)), dma((QCH,)),
        dma((QCH, nx)), dma((QCH, nx)), dma((QCH,)), dma((QCH,)),
    ]
    vmem = pl.BlockSpec(memory_space=pltpu.VMEM)
    out = jax.ShapeDtypeStruct((k, width), f32)
    x, total = pl.pallas_call(
        functools.partial(_fused_kernel, n_feat, n_rows, rh, cw),
        out_shape=(out, out),
        in_specs=[vmem] * 6,
        out_specs=(vmem, vmem),
        scratch_shapes=[
            pltpu.VMEM((k, s), f32),
            pltpu.VMEM((k, s), f32),
            pltpu.VMEM((k, s), jnp.bfloat16),
            pltpu.VMEM((k, width), f32),
        ] + feat_scr + rows_scr,
        compiler_params=pltpu.CompilerParams(
            collective_id=0, has_side_effects=True, vmem_limit_bytes=60 * 1024 * 1024),
    )(design, labels, x0, dual, cz, prm)
    return pl.pallas_call(
        functools.partial(_final_kernel, n_rows),
        out_shape=(out, out, out),
        in_specs=[vmem] * 4,
        out_specs=(vmem, vmem, vmem),
    )(x, total, dual, prm)


def per_device(n_rows, n_feat, design, labels, local_x, dual_u, consensus_z, step_size, rho, penalty):
    prm = jnp.stack([step_size, rho, penalty / (rho * n_rows)], axis=1)
    x, new_z, new_u = _fused(n_rows, n_feat, design, labels, local_x[0], dual_u[0],
                             consensus_z, prm)
    return (x[None], new_z, new_u[None])


def solution(mesh):
    in_specs = (
        P("rows", "feat"),
        P(None, "rows"),
        P("rows", None, "feat"),
        P("rows", None, "feat"),
        P(None, "feat"),
        P(),
        P(),
        P(),
    )
    out_specs = (P("rows", None, "feat"), P(None, "feat"), P("rows", None, "feat"))
    fn = functools.partial(per_device, mesh.shape["rows"], mesh.shape["feat"])
    return jax.shard_map(
        fn, mesh=mesh, in_specs=in_specs, out_specs=out_specs, check_vma=False
    )
```

```python
import functools

import jax
import jax.numpy as jnp
from jax import lax
from jax.experimental import pallas as pl
from jax.experimental.pallas import tpu as pltpu
from jax.sharding import PartitionSpec as P

MESH = pl.DeviceIdType.MESH
AXES = ("rows", "feat")
TILE = 512
QCH = 8


def _device(axis, peer):
    return tuple(peer if a == axis else lax.axis_index(a) for a in AXES)


def _rcopy(axis, src, dst, ss, rs, p):
    return pltpu.make_async_remote_copy(
        src_ref=src, dst_ref=dst, send_sem=ss, recv_sem=rs,
        device_id=_device(axis, p), device_id_type=MESH)


def _feat_allreduce(n, rh, cw, x_ref, o_ref, recv, gath, ss1, rs1, ss2, rs2):
    me = lax.axis_index("feat")
    peers = [lax.rem(me + d, n) for d in range(n)]
    srcs = [lax.rem(me + n - d, n) for d in range(n)]
    cblocks = x_ref.shape[1] // cw

    def block(ref, p):
        r = pl.multiple_of((p // cblocks) * rh, 8)
        c = pl.multiple_of((p % cblocks) * cw, 128)
        return ref.at[pl.ds(r, rh), pl.ds(c, cw)]

    sends = []
    for d in range(1, n):
        c = _rcopy("feat", block(x_ref, peers[d]), recv.at[me], ss1.at[d], rs1.at[d], peers[d])
        c.start()
        sends.append(c)
    acc = block(x_ref, me)[...]
    for d in range(1, n):
        _rcopy("feat", recv.at[srcs[d]], recv.at[srcs[d]], ss1.at[d], rs1.at[d], srcs[d]).wait_recv()
        acc = acc + recv[srcs[d]]
    gath[me] = acc
    sends2 = []
    for d in range(1, n):
        c = _rcopy("feat", gath.at[me], gath.at[me], ss2.at[d], rs2.at[d], peers[d])
        c.start()
        sends2.append(c)
    for c in sends:
        c.wait_send()
    for d in range(1, n):
        _rcopy("feat", gath.at[srcs[d]], gath.at[srcs[d]], ss2.at[d], rs2.at[d], srcs[d]).wait_recv()
    for c in sends2:
        c.wait_send()
    for p in range(n):
        r, c = (p // cblocks) * rh, (p % cblocks) * cw
        o_ref[r:r + rh, c:c + cw] = gath[p]


def _rows_allreduce(nx, x_ref, o_ref, ra, hbuf, rb, rc, gb, ge,
                    ssa, rsa, ssb, rsb, ssc, rsc, ssd, rsd, sse, rse):
    r = lax.axis_index("rows")
    n = 4 * nx
    half, blk = x_ref.shape[0] // 2, x_ref.shape[0] // (2 * nx)
    wq = x_ref.shape[1] // QCH
    c = lax.rem(r, 2)
    xi = lax.rem(r // 2, nx)
    base = r - 2 * xi
    partner = r + 1 - 2 * c
    xpeers = [base + 2 * lax.rem(xi + d, nx) for d in range(nx)]
    xsrcs = [lax.rem(xi + nx - d, nx) for d in range(nx)]
    zpeer = lax.rem(r + 2 * nx, n)
    rcopy = functools.partial(_rcopy, "rows")
    mine = pl.multiple_of(c * half, 8)
    other = pl.multiple_of((1 - c) * half, 8)

    def cols(q):
        return pl.ds(q * wq, wq)

    def rows_of(j):
        return pl.ds(pl.multiple_of(j * blk, 8), blk)

    a = []
    for q in range(QCH):
        cp = rcopy(x_ref.at[pl.ds(other, half), cols(q)], ra.at[:, cols(q)], ssa.at[q], rsa.at[q], partner)
        cp.start()
        a.append(cp)
    bs = []
    for q in range(QCH):
        a[q].wait()
        hbuf[:, cols(q)] = x_ref[pl.ds(mine, half), cols(q)] + ra[:, cols(q)]
        for d in range(1, nx):
            j = lax.rem(xi + d, nx)
            cp = rcopy(hbuf.at[rows_of(j), cols(q)], rb.at[xi, :, cols(q)],
                       ssb.at[q, d], rsb.at[q, d], xpeers[d])
            cp.start()
            bs.append(cp)
    cz = []
    for q in range(QCH):
        acc = hbuf[rows_of(xi), cols(q)]
        for d in range(1, nx):
            rcopy(rb.at[xsrcs[d], :, cols(q)], rb.at[xsrcs[d], :, cols(q)],
                  ssb.at[q, d], rsb.at[q, d], xpeers[d]).wait_recv()
            acc = acc + rb[xsrcs[d], :, cols(q)]
        gb[xi, :, cols(q)] = acc
        cp = rcopy(gb.at[xi, :, cols(q)], rc.at[:, cols(q)], ssc.at[q], rsc.at[q], zpeer)
        cp.start()
        cz.append(cp)
    ds_ = []
    for q in range(QCH):
        cz[q].wait()
        gb[xi, :, cols(q)] = gb[xi, :, cols(q)] + rc[:, cols(q)]
        for d in range(1, nx):
            cp = rcopy(gb.at[xi, :, cols(q)], gb.at[xi, :, cols(q)], ssd.at[q, d], rsd.at[q, d], xpeers[d])
            cp.start()
            ds_.append(cp)
    e = []
    for q in range(QCH):
        for d in range(1, nx):
            rcopy(gb.at[xsrcs[d], :, cols(q)], gb.at[xsrcs[d], :, cols(q)],
                  ssd.at[q, d], rsd.at[q, d], xpeers[d]).wait_recv()
        cp = rcopy(gb.at[:, :, cols(q)], ge.at[:, :, cols(q)], sse.at[q], rse.at[q], partner)
        cp.start()
        e.append(cp)
    for cp in bs + ds_:
        cp.wait_send()
    for q in range(QCH):
        e[q].wait()
        for j in range(nx):
            o_ref[pl.ds(pl.multiple_of(mine + j * blk, 8), blk), cols(q)] = gb[j, :, cols(q)]
            o_ref[pl.ds(pl.multiple_of(other + j * blk, 8), blk), cols(q)] = ge[j, :, cols(q)]


def _fused_kernel(nf, nr, rh, cw, design_hbm, lab, x0, dual_hbm, cz_hbm, prm,
                  ox, ot, pbuf, mbuf, rbuf, sbuf, design, dual, cz, lsem, *scratch):
    loads = [pltpu.make_async_copy(src, dst, lsem.at[i])
             for i, (src, dst) in enumerate([(design_hbm, design), (dual_hbm, dual), (cz_hbm, cz)])]
    for cp in loads:
        cp.start()
    feat_scr = scratch[:12]
    rows_scr = scratch[12:]
    nx = nr // 4

    me_f = lax.axis_index("feat")
    r = lax.axis_index("rows")
    fpeers = [lax.rem(me_f + d, nf) for d in range(1, nf)]
    c = lax.rem(r, 2)
    xi = lax.rem(r // 2, nx)
    rpeers = [r + 1 - 2 * c, lax.rem(r + 2 * nx, nr)]
    rpeers += [r - 2 * xi + 2 * lax.rem(xi + d, nx) for d in range(1, nx)]

    barrier = pltpu.get_barrier_semaphore()
    for p in fpeers:
        pl.semaphore_signal(barrier, inc=1, device_id=_device("feat", p), device_id_type=MESH)
    for p in rpeers:
        pl.semaphore_signal(barrier, inc=1, device_id=_device("rows", p), device_id_type=MESH)
    pl.semaphore_wait(barrier, len(fpeers) + len(rpeers))

    eta = prm[:, 0:1]
    rho = prm[:, 1:2]
    ox[...] = x0[...]
    ntile = design.shape[1] // TILE
    loads[0].wait()
    for turn in range(2):
        def margin_body(k, acc):
            cols = pl.ds(pl.multiple_of(k * TILE, TILE), TILE)
            xk = ox[:, cols].astype(jnp.bfloat16)
            return acc + lax.dot_general(
                xk, design[:, cols], (((1,), (1,)), ((), ())),
                preferred_element_type=jnp.float32)

        pbuf[...] = lax.fori_loop(0, ntile, margin_body, jnp.zeros(pbuf.shape, jnp.float32))
        _feat_allreduce(nf, rh, cw, pbuf, mbuf, *feat_scr[turn * 6:(turn + 1) * 6])
        sign = lab[...].astype(jnp.float32)
        rbuf[...] = (sign * jax.nn.sigmoid(-sign * mbuf[...])).astype(jnp.bfloat16)
        if turn == 0:
            loads[1].wait()
            loads[2].wait()

        def grad_body(j, carry):
            cols = pl.ds(pl.multiple_of(j * TILE, TILE), TILE)
            g = jnp.dot(rbuf[...], design[:, cols], preferred_element_type=jnp.float32)
            x = ox[:, cols]
            ox[:, cols] = x - eta * (rho * (x - cz[:, cols] + dual[:, cols]) - g)
            return carry

        lax.fori_loop(0, ntile, grad_body, 0)

    sbuf[...] = ox[...] + dual[...]
    _rows_allreduce(nx, sbuf, ot, *rows_scr)


def _final_kernel(nr, x, total, dual, prm, ox, oz, ou):
    lim = prm[:, 2:3]
    mean = total[...] / nr
    new_z = mean - jnp.clip(mean, -lim, lim)
    ox[...] = x[...]
    oz[...] = new_z
    ou[...] = dual[...] + x[...] - new_z


def _fused(n_rows, n_feat, design, labels, x0, dual, cz, prm):
    k, width = x0.shape
    s = design.shape[0]
    rblocks = min(k // 8, n_feat)
    rh, cw = k // rblocks, s * rblocks // n_feat
    nx = n_rows // 4
    half, blk = k // 2, k // (2 * nx)
    f32 = jnp.float32
    dma = pltpu.SemaphoreType.DMA
    feat_scr = []
    for _ in range(2):
        feat_scr += [pltpu.VMEM((n_feat, rh, cw), f32), pltpu.VMEM((n_feat, rh, cw), f32)]
        feat_scr += [dma((n_feat,)) for _ in range(4)]
    rows_scr = [
        pltpu.VMEM((half, width), f32),
        pltpu.VMEM((half, width), f32),
        pltpu.VMEM((nx, blk, width), f32),
        pltpu.VMEM((blk, width), f32),
        pltpu.VMEM((nx, blk, width), f32),
        pltpu.VMEM((nx, blk, width), f32),
        dma((QCH,)), dma((QCH,)), dma((QCH, nx)), dma((QCH, nx)), dma((QCH,)), dma((QCH,)),
        dma((QCH, nx)), dma((QCH, nx)), dma((QCH,)), dma((QCH,)),
    ]
    vmem = pl.BlockSpec(memory_space=pltpu.VMEM)
    hbm = pl.BlockSpec(memory_space=pl.ANY)
    out = jax.ShapeDtypeStruct((k, width), f32)
    x, total = pl.pallas_call(
        functools.partial(_fused_kernel, n_feat, n_rows, rh, cw),
        out_shape=(out, out),
        in_specs=[hbm, vmem, vmem, hbm, hbm, vmem],
        out_specs=(vmem, vmem),
        scratch_shapes=[
            pltpu.VMEM((k, s), f32),
            pltpu.VMEM((k, s), f32),
            pltpu.VMEM((k, s), jnp.bfloat16),
            pltpu.VMEM((k, width), f32),
            pltpu.VMEM(design.shape, design.dtype),
            pltpu.VMEM((k, width), f32),
            pltpu.VMEM((k, width), f32),
            dma((3,)),
        ] + feat_scr + rows_scr,
        compiler_params=pltpu.CompilerParams(
            collective_id=0, has_side_effects=True, vmem_limit_bytes=60 * 1024 * 1024),
    )(design, labels, x0, dual, cz, prm)
    tile = pl.BlockSpec((k, 2 * TILE), lambda j: (0, j))
    return pl.pallas_call(
        functools.partial(_final_kernel, n_rows),
        out_shape=(out, out, out),
        grid=(width // (2 * TILE),),
        in_specs=[tile, tile, tile, pl.BlockSpec(prm.shape, lambda j: (0, 0))],
        out_specs=(tile, tile, tile),
    )(x, total, dual, prm)


def per_device(n_rows, n_feat, design, labels, local_x, dual_u, consensus_z, step_size, rho, penalty):
    prm = jnp.stack([step_size, rho, penalty / (rho * n_rows)], axis=1)
    x, new_z, new_u = _fused(n_rows, n_feat, design, labels, local_x[0], dual_u[0],
                             consensus_z, prm)
    return (x[None], new_z, new_u[None])


def solution(mesh):
    in_specs = (
        P("rows", "feat"),
        P(None, "rows"),
        P("rows", None, "feat"),
        P("rows", None, "feat"),
        P(None, "feat"),
        P(),
        P(),
        P(),
    )
    out_specs = (P("rows", None, "feat"), P(None, "feat"), P("rows", None, "feat"))
    fn = functools.partial(per_device, mesh.shape["rows"], mesh.shape["feat"])
    return jax.shard_map(
        fn, mesh=mesh, in_specs=in_specs, out_specs=out_specs, check_vma=False
    )
```

```python
import functools

import jax
import jax.numpy as jnp
from jax import lax
from jax.experimental import pallas as pl
from jax.experimental.pallas import tpu as pltpu
from jax.sharding import PartitionSpec as P

MESH = pl.DeviceIdType.MESH
AXES = ("rows", "feat")
TILE = 512
QCH = 8


def _device(axis, peer):
    return tuple(peer if a == axis else lax.axis_index(a) for a in AXES)


def _rcopy(axis, src, dst, ss, rs, p):
    return pltpu.make_async_remote_copy(
        src_ref=src, dst_ref=dst, send_sem=ss, recv_sem=rs,
        device_id=_device(axis, p), device_id_type=MESH)


def _feat_allreduce(n, rh, cw, x_ref, o_ref, recv, gath, ss1, rs1, ss2, rs2):
    me = lax.axis_index("feat")
    peers = [lax.rem(me + d, n) for d in range(n)]
    srcs = [lax.rem(me + n - d, n) for d in range(n)]
    cblocks = x_ref.shape[1] // cw

    def block(ref, p):
        r = pl.multiple_of((p // cblocks) * rh, 8)
        c = pl.multiple_of((p % cblocks) * cw, 128)
        return ref.at[pl.ds(r, rh), pl.ds(c, cw)]

    sends = []
    for d in range(1, n):
        c = _rcopy("feat", block(x_ref, peers[d]), recv.at[me], ss1.at[d], rs1.at[d], peers[d])
        c.start()
        sends.append(c)
    acc = block(x_ref, me)[...]
    for d in range(1, n):
        _rcopy("feat", recv.at[srcs[d]], recv.at[srcs[d]], ss1.at[d], rs1.at[d], srcs[d]).wait_recv()
        acc = acc + recv[srcs[d]]
    gath[me] = acc
    sends2 = []
    for d in range(1, n):
        c = _rcopy("feat", gath.at[me], gath.at[me], ss2.at[d], rs2.at[d], peers[d])
        c.start()
        sends2.append(c)
    for c in sends:
        c.wait_send()
    for d in range(1, n):
        _rcopy("feat", gath.at[srcs[d]], gath.at[srcs[d]], ss2.at[d], rs2.at[d], srcs[d]).wait_recv()
    for c in sends2:
        c.wait_send()
    for p in range(n):
        r, c = (p // cblocks) * rh, (p % cblocks) * cw
        o_ref[r:r + rh, c:c + cw] = gath[p]


def _rows_allreduce(nx, x_ref, o_ref, ra, hbuf, rb, rc, gb, ge,
                    ssa, rsa, ssb, rsb, ssc, rsc, ssd, rsd, sse, rse):
    r = lax.axis_index("rows")
    n = 4 * nx
    half, blk = x_ref.shape[0] // 2, x_ref.shape[0] // (2 * nx)
    wq = x_ref.shape[1] // QCH
    c = lax.rem(r, 2)
    xi = lax.rem(r // 2, nx)
    base = r - 2 * xi
    partner = r + 1 - 2 * c
    xpeers = [base + 2 * lax.rem(xi + d, nx) for d in range(nx)]
    xsrcs = [lax.rem(xi + nx - d, nx) for d in range(nx)]
    zpeer = lax.rem(r + 2 * nx, n)
    rcopy = functools.partial(_rcopy, "rows")
    mine = pl.multiple_of(c * half, 8)
    other = pl.multiple_of((1 - c) * half, 8)

    def cols(q):
        return pl.ds(q * wq, wq)

    def rows_of(j):
        return pl.ds(pl.multiple_of(j * blk, 8), blk)

    a = [rcopy(x_ref.at[pl.ds(other, half), cols(q)], ra.at[:, cols(q)], ssa.at[q], rsa.at[q], partner)
         for q in range(QCH)]
    bs = []
    for q in range(QCH):
        a[q].wait()
        hbuf[:, cols(q)] = x_ref[pl.ds(mine, half), cols(q)] + ra[:, cols(q)]
        for d in range(1, nx):
            j = lax.rem(xi + d, nx)
            cp = rcopy(hbuf.at[rows_of(j), cols(q)], rb.at[xi, :, cols(q)],
                       ssb.at[q, d], rsb.at[q, d], xpeers[d])
            cp.start()
            bs.append(cp)
    cz = []
    for q in range(QCH):
        acc = hbuf[rows_of(xi), cols(q)]
        for d in range(1, nx):
            rcopy(rb.at[xsrcs[d], :, cols(q)], rb.at[xsrcs[d], :, cols(q)],
                  ssb.at[q, d], rsb.at[q, d], xpeers[d]).wait_recv()
            acc = acc + rb[xsrcs[d], :, cols(q)]
        gb[xi, :, cols(q)] = acc
        cp = rcopy(gb.at[xi, :, cols(q)], rc.at[:, cols(q)], ssc.at[q], rsc.at[q], zpeer)
        cp.start()
        cz.append(cp)
    ds_ = []
    for q in range(QCH):
        cz[q].wait()
        gb[xi, :, cols(q)] = gb[xi, :, cols(q)] + rc[:, cols(q)]
        for d in range(1, nx):
            cp = rcopy(gb.at[xi, :, cols(q)], gb.at[xi, :, cols(q)], ssd.at[q, d], rsd.at[q, d], xpeers[d])
            cp.start()
            ds_.append(cp)
    e = []
    for q in range(QCH):
        for d in range(1, nx):
            rcopy(gb.at[xsrcs[d], :, cols(q)], gb.at[xsrcs[d], :, cols(q)],
                  ssd.at[q, d], rsd.at[q, d], xpeers[d]).wait_recv()
        cp = rcopy(gb.at[:, :, cols(q)], ge.at[:, :, cols(q)], sse.at[q], rse.at[q], partner)
        cp.start()
        e.append(cp)
    for cp in bs + ds_:
        cp.wait_send()
    for q in range(QCH):
        e[q].wait()
        for j in range(nx):
            o_ref[pl.ds(pl.multiple_of(mine + j * blk, 8), blk), cols(q)] = gb[j, :, cols(q)]
            o_ref[pl.ds(pl.multiple_of(other + j * blk, 8), blk), cols(q)] = ge[j, :, cols(q)]


def _fused_kernel(nf, nr, rh, cw, design_hbm, lab, x0, dual_hbm, cz_hbm, prm,
                  ox, ot, pbuf, mbuf, rbuf, sbuf, design, dual, cz, lsem, *scratch):
    loads = [pltpu.make_async_copy(src, dst, lsem.at[i])
             for i, (src, dst) in enumerate([(design_hbm, design), (dual_hbm, dual), (cz_hbm, cz)])]
    for cp in loads:
        cp.start()
    feat_scr = scratch[:12]
    rows_scr = scratch[12:]
    nx = nr // 4

    me_f = lax.axis_index("feat")
    r = lax.axis_index("rows")
    fpeers = [lax.rem(me_f + d, nf) for d in range(1, nf)]
    c = lax.rem(r, 2)
    xi = lax.rem(r // 2, nx)
    rpeers = [r + 1 - 2 * c, lax.rem(r + 2 * nx, nr)]
    rpeers += [r - 2 * xi + 2 * lax.rem(xi + d, nx) for d in range(1, nx)]

    barrier = pltpu.get_barrier_semaphore()
    for p in fpeers:
        pl.semaphore_signal(barrier, inc=1, device_id=_device("feat", p), device_id_type=MESH)
    for p in rpeers:
        pl.semaphore_signal(barrier, inc=1, device_id=_device("rows", p), device_id_type=MESH)

    eta = prm[:, 0:1]
    rho = prm[:, 1:2]
    ox[...] = x0[...]
    ntile = design.shape[1] // TILE
    loads[0].wait()
    for turn in range(2):
        def margin_body(k, acc):
            cols = pl.ds(pl.multiple_of(k * TILE, TILE), TILE)
            xk = ox[:, cols].astype(jnp.bfloat16)
            return acc + lax.dot_general(
                xk, design[:, cols], (((1,), (1,)), ((), ())),
                preferred_element_type=jnp.float32)

        pbuf[...] = lax.fori_loop(0, ntile, margin_body, jnp.zeros(pbuf.shape, jnp.float32))
        if turn == 0:
            pl.semaphore_wait(barrier, len(fpeers) + len(rpeers))
        _feat_allreduce(nf, rh, cw, pbuf, mbuf, *feat_scr[turn * 6:(turn + 1) * 6])
        sign = lab[...].astype(jnp.float32)
        rbuf[...] = (sign * jax.nn.sigmoid(-sign * mbuf[...])).astype(jnp.bfloat16)
        if turn == 0:
            loads[1].wait()
            loads[2].wait()

        def grad_body(j, carry):
            cols = pl.ds(pl.multiple_of(j * TILE, TILE), TILE)
            g = jnp.dot(rbuf[...], design[:, cols], preferred_element_type=jnp.float32)
            x = ox[:, cols]
            x = x - eta * (rho * (x - cz[:, cols] + dual[:, cols]) - g)
            ox[:, cols] = x
            if turn == 1:
                sbuf[:, cols] = x + dual[:, cols]
                half = x.shape[0] // 2
                other = pl.multiple_of((1 - lax.rem(r, 2)) * half, 8)
                _rcopy("rows", sbuf.at[pl.ds(other, half), cols], rows_scr[0].at[:, cols],
                       rows_scr[6].at[j], rows_scr[7].at[j], rpeers[0]).start()
            return carry

        lax.fori_loop(0, ntile, grad_body, 0)

    _rows_allreduce(nx, sbuf, ot, *rows_scr)


def _final_kernel(nr, x, total, dual, prm, ox, oz, ou):
    lim = prm[:, 2:3]
    mean = total[...] / nr
    new_z = mean - jnp.clip(mean, -lim, lim)
    ox[...] = x[...]
    oz[...] = new_z
    ou[...] = dual[...] + x[...] - new_z


def _fused(n_rows, n_feat, design, labels, x0, dual, cz, prm):
    k, width = x0.shape
    s = design.shape[0]
    rblocks = min(k // 8, n_feat)
    rh, cw = k // rblocks, s * rblocks // n_feat
    nx = n_rows // 4
    half, blk = k // 2, k // (2 * nx)
    f32 = jnp.float32
    dma = pltpu.SemaphoreType.DMA
    feat_scr = []
    for _ in range(2):
        feat_scr += [pltpu.VMEM((n_feat, rh, cw), f32), pltpu.VMEM((n_feat, rh, cw), f32)]
        feat_scr += [dma((n_feat,)) for _ in range(4)]
    rows_scr = [
        pltpu.VMEM((half, width), f32),
        pltpu.VMEM((half, width), f32),
        pltpu.VMEM((nx, blk, width), f32),
        pltpu.VMEM((blk, width), f32),
        pltpu.VMEM((nx, blk, width), f32),
        pltpu.VMEM((nx, blk, width), f32),
        dma((QCH,)), dma((QCH,)), dma((QCH, nx)), dma((QCH, nx)), dma((QCH,)), dma((QCH,)),
        dma((QCH, nx)), dma((QCH, nx)), dma((QCH,)), dma((QCH,)),
    ]
    vmem = pl.BlockSpec(memory_space=pltpu.VMEM)
    hbm = pl.BlockSpec(memory_space=pl.ANY)
    out = jax.ShapeDtypeStruct((k, width), f32)
    x, total = pl.pallas_call(
        functools.partial(_fused_kernel, n_feat, n_rows, rh, cw),
        out_shape=(out, out),
        in_specs=[hbm, vmem, vmem, hbm, hbm, vmem],
        out_specs=(vmem, vmem),
        scratch_shapes=[
            pltpu.VMEM((k, s), f32),
            pltpu.VMEM((k, s), f32),
            pltpu.VMEM((k, s), jnp.bfloat16),
            pltpu.VMEM((k, width), f32),
            pltpu.VMEM(design.shape, design.dtype),
            pltpu.VMEM((k, width), f32),
            pltpu.VMEM((k, width), f32),
            dma((3,)),
        ] + feat_scr + rows_scr,
        compiler_params=pltpu.CompilerParams(
            collective_id=0, has_side_effects=True, vmem_limit_bytes=60 * 1024 * 1024),
    )(design, labels, x0, dual, cz, prm)
    tile = pl.BlockSpec((k, 2 * TILE), lambda j: (0, j))
    return pl.pallas_call(
        functools.partial(_final_kernel, n_rows),
        out_shape=(out, out, out),
        grid=(width // (2 * TILE),),
        in_specs=[tile, tile, tile, pl.BlockSpec(prm.shape, lambda j: (0, 0))],
        out_specs=(tile, tile, tile),
    )(x, total, dual, prm)


def per_device(n_rows, n_feat, design, labels, local_x, dual_u, consensus_z, step_size, rho, penalty):
    prm = jnp.stack([step_size, rho, penalty / (rho * n_rows)], axis=1)
    x, new_z, new_u = _fused(n_rows, n_feat, design, labels, local_x[0], dual_u[0],
                             consensus_z, prm)
    return (x[None], new_z, new_u[None])


def solution(mesh):
    in_specs = (
        P("rows", "feat"),
        P(None, "rows"),
        P("rows", None, "feat"),
        P("rows", None, "feat"),
        P(None, "feat"),
        P(),
        P(),
        P(),
    )
    out_specs = (P("rows", None, "feat"), P(None, "feat"), P("rows", None, "feat"))
    fn = functools.partial(per_device, mesh.shape["rows"], mesh.shape["feat"])
    return jax.shard_map(
        fn, mesh=mesh, in_specs=in_specs, out_specs=out_specs, check_vma=False
    )
```

```python
import functools

import jax
import jax.numpy as jnp
from jax import lax
from jax.experimental import pallas as pl
from jax.experimental.pallas import tpu as pltpu
from jax.sharding import PartitionSpec as P

MESH = pl.DeviceIdType.MESH
AXES = ("rows", "feat")
TILE = 512
QCH = 8


def _device(axis, peer):
    return tuple(peer if a == axis else lax.axis_index(a) for a in AXES)


def _rcopy(axis, src, dst, ss, rs, p):
    return pltpu.make_async_remote_copy(
        src_ref=src, dst_ref=dst, send_sem=ss, recv_sem=rs,
        device_id=_device(axis, p), device_id_type=MESH)


def _feat_block(rh, cw, cblocks, ref, p):
    r = pl.multiple_of((p // cblocks) * rh, 8)
    c = pl.multiple_of((p % cblocks) * cw, 128)
    return ref.at[pl.ds(r, rh), pl.ds(c, cw)]


def _feat_send(n, rh, cw, x_ref, recv, ss1, rs1, h):
    me = lax.axis_index("feat")
    cblocks = x_ref.shape[1] // cw
    for p in range(h, n, cblocks):
        @pl.when(me != p)
        def _():
            _rcopy("feat", _feat_block(rh, cw, cblocks, x_ref, p), recv.at[me],
                   ss1.at[p], rs1.at[me], p).start()


def _feat_finish(n, rh, cw, x_ref, o_ref, recv, gath, ss1, rs1, ss2, rs2):
    me = lax.axis_index("feat")
    peers = [lax.rem(me + d, n) for d in range(n)]
    srcs = [lax.rem(me + n - d, n) for d in range(n)]
    cblocks = x_ref.shape[1] // cw
    acc = _feat_block(rh, cw, cblocks, x_ref, me)[...]
    for d in range(1, n):
        _rcopy("feat", recv.at[srcs[d]], recv.at[srcs[d]], ss1.at[0], rs1.at[srcs[d]], srcs[d]).wait_recv()
        acc = acc + recv[srcs[d]]
    gath[me] = acc
    sends2 = []
    for d in range(1, n):
        c = _rcopy("feat", gath.at[me], gath.at[me], ss2.at[d], rs2.at[d], peers[d])
        c.start()
        sends2.append(c)
    for p in range(n):
        @pl.when(me != p)
        def _():
            _rcopy("feat", _feat_block(rh, cw, cblocks, x_ref, p), recv.at[me],
                   ss1.at[p], rs1.at[me], p).wait_send()
    for d in range(1, n):
        _rcopy("feat", gath.at[srcs[d]], gath.at[srcs[d]], ss2.at[d], rs2.at[d], srcs[d]).wait_recv()
    for c in sends2:
        c.wait_send()
    for p in range(n):
        r, c = (p // cblocks) * rh, (p % cblocks) * cw
        o_ref[r:r + rh, c:c + cw] = gath[p]


def _rows_allreduce(nx, x_ref, o_ref, ra, hbuf, rb, rc, gb, ge,
                    ssa, rsa, ssb, rsb, ssc, rsc, ssd, rsd, sse, rse):
    r = lax.axis_index("rows")
    n = 4 * nx
    half, blk = x_ref.shape[0] // 2, x_ref.shape[0] // (2 * nx)
    wq = x_ref.shape[1] // QCH
    c = lax.rem(r, 2)
    xi = lax.rem(r // 2, nx)
    base = r - 2 * xi
    partner = r + 1 - 2 * c
    xpeers = [base + 2 * lax.rem(xi + d, nx) for d in range(nx)]
    xsrcs = [lax.rem(xi + nx - d, nx) for d in range(nx)]
    zpeer = lax.rem(r + 2 * nx, n)
    rcopy = functools.partial(_rcopy, "rows")
    mine = pl.multiple_of(c * half, 8)
    other = pl.multiple_of((1 - c) * half, 8)

    def cols(q):
        return pl.ds(q * wq, wq)

    def rows_of(j):
        return pl.ds(pl.multiple_of(j * blk, 8), blk)

    a = [rcopy(x_ref.at[pl.ds(other, half), cols(q)], ra.at[:, cols(q)], ssa.at[q], rsa.at[q], partner)
         for q in range(QCH)]
    bs = []
    for q in range(QCH):
        a[q].wait()
        hbuf[:, cols(q)] = x_ref[pl.ds(mine, half), cols(q)] + ra[:, cols(q)]
        for d in range(1, nx):
            j = lax.rem(xi + d, nx)
            cp = rcopy(hbuf.at[rows_of(j), cols(q)], rb.at[xi, :, cols(q)],
                       ssb.at[q, d], rsb.at[q, d], xpeers[d])
            cp.start()
            bs.append(cp)
    cz = []
    for q in range(QCH):
        acc = hbuf[rows_of(xi), cols(q)]
        for d in range(1, nx):
            rcopy(rb.at[xsrcs[d], :, cols(q)], rb.at[xsrcs[d], :, cols(q)],
                  ssb.at[q, d], rsb.at[q, d], xpeers[d]).wait_recv()
            acc = acc + rb[xsrcs[d], :, cols(q)]
        gb[xi, :, cols(q)] = acc
        cp = rcopy(gb.at[xi, :, cols(q)], rc.at[:, cols(q)], ssc.at[q], rsc.at[q], zpeer)
        cp.start()
        cz.append(cp)
    ds_ = []
    for q in range(QCH):
        cz[q].wait()
        gb[xi, :, cols(q)] = gb[xi, :, cols(q)] + rc[:, cols(q)]
        for d in range(1, nx):
            cp = rcopy(gb.at[xi, :, cols(q)], gb.at[xi, :, cols(q)], ssd.at[q, d], rsd.at[q, d], xpeers[d])
            cp.start()
            ds_.append(cp)
    e = []
    for q in range(QCH):
        for d in range(1, nx):
            rcopy(gb.at[xsrcs[d], :, cols(q)], gb.at[xsrcs[d], :, cols(q)],
                  ssd.at[q, d], rsd.at[q, d], xpeers[d]).wait_recv()
        cp = rcopy(gb.at[:, :, cols(q)], ge.at[:, :, cols(q)], sse.at[q], rse.at[q], partner)
        cp.start()
        e.append(cp)
    for cp in bs + ds_:
        cp.wait_send()
    for q in range(QCH):
        e[q].wait()
        for j in range(nx):
            o_ref[pl.ds(pl.multiple_of(mine + j * blk, 8), blk), cols(q)] = gb[j, :, cols(q)]
            o_ref[pl.ds(pl.multiple_of(other + j * blk, 8), blk), cols(q)] = ge[j, :, cols(q)]


def _fused_kernel(nf, nr, rh, cw, design_hbm, lab, x0, dual_hbm, cz_hbm, prm,
                  ox, ot, pbuf, mbuf, rbuf, sbuf, design, dual, cz, lsem, *scratch):
    loads = [pltpu.make_async_copy(src, dst, lsem.at[i])
             for i, (src, dst) in enumerate([(design_hbm, design), (dual_hbm, dual), (cz_hbm, cz)])]
    for cp in loads:
        cp.start()
    feat_scr = scratch[:12]
    rows_scr = scratch[12:]
    nx = nr // 4

    me_f = lax.axis_index("feat")
    r = lax.axis_index("rows")
    fpeers = [lax.rem(me_f + d, nf) for d in range(1, nf)]
    c = lax.rem(r, 2)
    xi = lax.rem(r // 2, nx)
    rpeers = [r + 1 - 2 * c, lax.rem(r + 2 * nx, nr)]
    rpeers += [r - 2 * xi + 2 * lax.rem(xi + d, nx) for d in range(1, nx)]

    barrier = pltpu.get_barrier_semaphore()
    for p in fpeers:
        pl.semaphore_signal(barrier, inc=1, device_id=_device("feat", p), device_id_type=MESH)
    for p in rpeers:
        pl.semaphore_signal(barrier, inc=1, device_id=_device("rows", p), device_id_type=MESH)

    eta = prm[:, 0:1]
    rho = prm[:, 1:2]
    ox[...] = x0[...]
    ntile = design.shape[1] // TILE
    cblocks = design.shape[0] // cw
    loads[0].wait()
    for turn in range(2):
        def margin_body(sc, k, acc):
            cols = pl.ds(pl.multiple_of(k * TILE, TILE), TILE)
            xk = ox[:, cols].astype(jnp.bfloat16)
            return acc + lax.dot_general(
                xk, design[sc, cols], (((1,), (1,)), ((), ())),
                preferred_element_type=jnp.float32)

        fs = feat_scr[turn * 6:(turn + 1) * 6]
        for h in range(cblocks):
            sc = pl.ds(h * cw, cw)
            pbuf[:, sc] = lax.fori_loop(
                0, ntile, functools.partial(margin_body, sc), jnp.zeros((pbuf.shape[0], cw), jnp.float32))
            if turn == 0 and h == 0:
                pl.semaphore_wait(barrier, len(fpeers) + len(rpeers))
            _feat_send(nf, rh, cw, pbuf, fs[0], fs[2], fs[3], h)
        _feat_finish(nf, rh, cw, pbuf, mbuf, *fs)
        sign = lab[...].astype(jnp.float32)
        rbuf[...] = (sign * jax.nn.sigmoid(-sign * mbuf[...])).astype(jnp.bfloat16)
        if turn == 0:
            loads[1].wait()
            loads[2].wait()

        def grad_body(j, carry):
            cols = pl.ds(pl.multiple_of(j * TILE, TILE), TILE)
            g = jnp.dot(rbuf[...], design[:, cols], preferred_element_type=jnp.float32)
            x = ox[:, cols]
            x = x - eta * (rho * (x - cz[:, cols] + dual[:, cols]) - g)
            ox[:, cols] = x
            if turn == 1:
                sbuf[:, cols] = x + dual[:, cols]
                half = x.shape[0] // 2
                other = pl.multiple_of((1 - lax.rem(r, 2)) * half, 8)
                _rcopy("rows", sbuf.at[pl.ds(other, half), cols], rows_scr[0].at[:, cols],
                       rows_scr[6].at[j], rows_scr[7].at[j], rpeers[0]).start()
            return carry

        lax.fori_loop(0, ntile, grad_body, 0)

    _rows_allreduce(nx, sbuf, ot, *rows_scr)


def _final_kernel(nr, x, total, dual, prm, ox, oz, ou):
    lim = prm[:, 2:3]
    mean = total[...] / nr
    new_z = mean - jnp.clip(mean, -lim, lim)
    ox[...] = x[...]
    oz[...] = new_z
    ou[...] = dual[...] + x[...] - new_z


def _fused(n_rows, n_feat, design, labels, x0, dual, cz, prm):
    k, width = x0.shape
    s = design.shape[0]
    rblocks = min(k // 8, n_feat)
    rh, cw = k // rblocks, s * rblocks // n_feat
    nx = n_rows // 4
    half, blk = k // 2, k // (2 * nx)
    f32 = jnp.float32
    dma = pltpu.SemaphoreType.DMA
    feat_scr = []
    for _ in range(2):
        feat_scr += [pltpu.VMEM((n_feat, rh, cw), f32), pltpu.VMEM((n_feat, rh, cw), f32)]
        feat_scr += [dma((n_feat,)) for _ in range(4)]
    rows_scr = [
        pltpu.VMEM((half, width), f32),
        pltpu.VMEM((half, width), f32),
        pltpu.VMEM((nx, blk, width), f32),
        pltpu.VMEM((blk, width), f32),
        pltpu.VMEM((nx, blk, width), f32),
        pltpu.VMEM((nx, blk, width), f32),
        dma((QCH,)), dma((QCH,)), dma((QCH, nx)), dma((QCH, nx)), dma((QCH,)), dma((QCH,)),
        dma((QCH, nx)), dma((QCH, nx)), dma((QCH,)), dma((QCH,)),
    ]
    vmem = pl.BlockSpec(memory_space=pltpu.VMEM)
    hbm = pl.BlockSpec(memory_space=pl.ANY)
    out = jax.ShapeDtypeStruct((k, width), f32)
    x, total = pl.pallas_call(
        functools.partial(_fused_kernel, n_feat, n_rows, rh, cw),
        out_shape=(out, out),
        in_specs=[hbm, vmem, vmem, hbm, hbm, vmem],
        out_specs=(vmem, vmem),
        scratch_shapes=[
            pltpu.VMEM((k, s), f32),
            pltpu.VMEM((k, s), f32),
            pltpu.VMEM((k, s), jnp.bfloat16),
            pltpu.VMEM((k, width), f32),
            pltpu.VMEM(design.shape, design.dtype),
            pltpu.VMEM((k, width), f32),
            pltpu.VMEM((k, width), f32),
            dma((3,)),
        ] + feat_scr + rows_scr,
        compiler_params=pltpu.CompilerParams(
            collective_id=0, has_side_effects=True, vmem_limit_bytes=60 * 1024 * 1024),
    )(design, labels, x0, dual, cz, prm)
    tile = pl.BlockSpec((k, 2 * TILE), lambda j: (0, j))
    return pl.pallas_call(
        functools.partial(_final_kernel, n_rows),
        out_shape=(out, out, out),
        grid=(width // (2 * TILE),),
        in_specs=[tile, tile, tile, pl.BlockSpec(prm.shape, lambda j: (0, 0))],
        out_specs=(tile, tile, tile),
    )(x, total, dual, prm)


def per_device(n_rows, n_feat, design, labels, local_x, dual_u, consensus_z, step_size, rho, penalty):
    prm = jnp.stack([step_size, rho, penalty / (rho * n_rows)], axis=1)
    x, new_z, new_u = _fused(n_rows, n_feat, design, labels, local_x[0], dual_u[0],
                             consensus_z, prm)
    return (x[None], new_z, new_u[None])


def solution(mesh):
    in_specs = (
        P("rows", "feat"),
        P(None, "rows"),
        P("rows", None, "feat"),
        P("rows", None, "feat"),
        P(None, "feat"),
        P(),
        P(),
        P(),
    )
    out_specs = (P("rows", None, "feat"), P(None, "feat"), P("rows", None, "feat"))
    fn = functools.partial(per_device, mesh.shape["rows"], mesh.shape["feat"])
    return jax.shard_map(
        fn, mesh=mesh, in_specs=in_specs, out_specs=out_specs, check_vma=False
    )
```

```python
import functools

import jax
import jax.numpy as jnp
from jax import lax
from jax.experimental import pallas as pl
from jax.experimental.pallas import tpu as pltpu
from jax.sharding import PartitionSpec as P

MESH = pl.DeviceIdType.MESH
AXES = ("rows", "feat")
TILE = 512
QCH = 8


def _device(axis, peer):
    return tuple(peer if a == axis else lax.axis_index(a) for a in AXES)


def _rcopy(axis, src, dst, ss, rs, p):
    return pltpu.make_async_remote_copy(
        src_ref=src, dst_ref=dst, send_sem=ss, recv_sem=rs,
        device_id=_device(axis, p), device_id_type=MESH)


def _feat_allreduce(n, rh, cw, x_ref, o_ref, recv, gath, ss1, rs1, ss2, rs2):
    me = lax.axis_index("feat")
    peers = [lax.rem(me + d, n) for d in range(n)]
    srcs = [lax.rem(me + n - d, n) for d in range(n)]
    cblocks = x_ref.shape[1] // cw

    def block(ref, p):
        r = pl.multiple_of((p // cblocks) * rh, 8)
        c = pl.multiple_of((p % cblocks) * cw, 128)
        return ref.at[pl.ds(r, rh), pl.ds(c, cw)]

    sends = []
    for d in range(1, n):
        c = _rcopy("feat", block(x_ref, peers[d]), recv.at[me], ss1.at[d], rs1.at[d], peers[d])
        c.start()
        sends.append(c)
    acc = block(x_ref, me)[...]
    for d in range(1, n):
        _rcopy("feat", recv.at[srcs[d]], recv.at[srcs[d]], ss1.at[d], rs1.at[d], srcs[d]).wait_recv()
        acc = acc + recv[srcs[d]]
    gath[me] = acc
    sends2 = []
    for d in range(1, n):
        c = _rcopy("feat", gath.at[me], gath.at[me], ss2.at[d], rs2.at[d], peers[d])
        c.start()
        sends2.append(c)
    for c in sends:
        c.wait_send()
    for d in range(1, n):
        _rcopy("feat", gath.at[srcs[d]], gath.at[srcs[d]], ss2.at[d], rs2.at[d], srcs[d]).wait_recv()
    for c in sends2:
        c.wait_send()
    for p in range(n):
        r, c = (p // cblocks) * rh, (p % cblocks) * cw
        o_ref[r:r + rh, c:c + cw] = gath[p]


def _rows_allreduce(nx, x_ref, o_ref, ra, hbuf, rb, rc, gb, ge,
                    ssa, rsa, ssb, rsb, ssc, rsc, ssd, rsd, sse, rse):
    r = lax.axis_index("rows")
    n = 4 * nx
    half, blk = x_ref.shape[0] // 2, x_ref.shape[0] // (2 * nx)
    wq = x_ref.shape[1] // QCH
    c = lax.rem(r, 2)
    xi = lax.rem(r // 2, nx)
    base = r - 2 * xi
    partner = r + 1 - 2 * c
    xpeers = [base + 2 * lax.rem(xi + d, nx) for d in range(nx)]
    xsrcs = [lax.rem(xi + nx - d, nx) for d in range(nx)]
    zpeer = lax.rem(r + 2 * nx, n)
    rcopy = functools.partial(_rcopy, "rows")
    mine = pl.multiple_of(c * half, 8)
    other = pl.multiple_of((1 - c) * half, 8)

    def cols(q):
        return pl.ds(q * wq, wq)

    def rows_of(j):
        return pl.ds(pl.multiple_of(j * blk, 8), blk)

    a = [rcopy(x_ref.at[pl.ds(other, half), cols(q)], ra.at[:, cols(q)], ssa.at[q], rsa.at[q], partner)
         for q in range(QCH)]
    bs = []
    for q in range(QCH):
        a[q].wait()
        hbuf[:, cols(q)] = x_ref[pl.ds(mine, half), cols(q)] + ra[:, cols(q)]
        for d in range(1, nx):
            j = lax.rem(xi + d, nx)
            cp = rcopy(hbuf.at[rows_of(j), cols(q)], rb.at[xi, :, cols(q)],
                       ssb.at[q, d], rsb.at[q, d], xpeers[d])
            cp.start()
            bs.append(cp)
    cz = []
    for q in range(QCH):
        acc = hbuf[rows_of(xi), cols(q)]
        for d in range(1, nx):
            rcopy(rb.at[xsrcs[d], :, cols(q)], rb.at[xsrcs[d], :, cols(q)],
                  ssb.at[q, d], rsb.at[q, d], xpeers[d]).wait_recv()
            acc = acc + rb[xsrcs[d], :, cols(q)]
        gb[xi, :, cols(q)] = acc
        cp = rcopy(gb.at[xi, :, cols(q)], rc.at[:, cols(q)], ssc.at[q], rsc.at[q], zpeer)
        cp.start()
        cz.append(cp)
    ds_ = []
    for q in range(QCH):
        cz[q].wait()
        gb[xi, :, cols(q)] = gb[xi, :, cols(q)] + rc[:, cols(q)]
        for d in range(1, nx):
            cp = rcopy(gb.at[xi, :, cols(q)], gb.at[xi, :, cols(q)], ssd.at[q, d], rsd.at[q, d], xpeers[d])
            cp.start()
            ds_.append(cp)
    e = []
    for q in range(QCH):
        for d in range(1, nx):
            rcopy(gb.at[xsrcs[d], :, cols(q)], gb.at[xsrcs[d], :, cols(q)],
                  ssd.at[q, d], rsd.at[q, d], xpeers[d]).wait_recv()
        cp = rcopy(gb.at[:, :, cols(q)], ge.at[:, :, cols(q)], sse.at[q], rse.at[q], partner)
        cp.start()
        e.append(cp)
    for cp in bs + ds_:
        cp.wait_send()
    for q in range(QCH):
        e[q].wait()
        for j in range(nx):
            o_ref[pl.ds(pl.multiple_of(mine + j * blk, 8), blk), cols(q)] = gb[j, :, cols(q)]
            o_ref[pl.ds(pl.multiple_of(other + j * blk, 8), blk), cols(q)] = ge[j, :, cols(q)]


def _fused_kernel(nf, nr, rh, cw, design_hbm, lab, x0, dual_hbm, cz_hbm, prm,
                  ox, ot, pbuf, mbuf, rbuf, sbuf, design, dual, cz, lsem, *scratch):
    loads = [pltpu.make_async_copy(src, dst, lsem.at[i])
             for i, (src, dst) in enumerate([(design_hbm, design), (dual_hbm, dual), (cz_hbm, cz)])]
    for cp in loads:
        cp.start()
    feat_scr = scratch[:12]
    rows_scr = scratch[12:]
    nx = nr // 4

    me_f = lax.axis_index("feat")
    r = lax.axis_index("rows")
    fpeers = [lax.rem(me_f + d, nf) for d in range(1, nf)]
    c = lax.rem(r, 2)
    xi = lax.rem(r // 2, nx)
    rpeers = [r + 1 - 2 * c, lax.rem(r + 2 * nx, nr)]
    rpeers += [r - 2 * xi + 2 * lax.rem(xi + d, nx) for d in range(1, nx)]

    barrier = pltpu.get_barrier_semaphore()
    for p in fpeers:
        pl.semaphore_signal(barrier, inc=1, device_id=_device("feat", p), device_id_type=MESH)
    for p in rpeers:
        pl.semaphore_signal(barrier, inc=1, device_id=_device("rows", p), device_id_type=MESH)

    eta = prm[:, 0:1]
    rho = prm[:, 1:2]
    ox[...] = x0[...]
    ntile = design.shape[1] // TILE
    loads[0].wait()
    for turn in range(2):
        def margin_body(k, acc):
            cols = pl.ds(pl.multiple_of(k * TILE, TILE), TILE)
            xk = ox[:, cols].astype(jnp.bfloat16)
            return acc + lax.dot_general(
                xk, design[:, cols], (((1,), (1,)), ((), ())),
                preferred_element_type=jnp.float32)

        if turn == 0:
            pbuf[...] = lax.fori_loop(0, ntile, margin_body, jnp.zeros(pbuf.shape, jnp.float32))
        if turn == 0:
            pl.semaphore_wait(barrier, len(fpeers) + len(rpeers))
        _feat_allreduce(nf, rh, cw, pbuf, mbuf, *feat_scr[turn * 6:(turn + 1) * 6])
        sign = lab[...].astype(jnp.float32)
        rbuf[...] = (sign * jax.nn.sigmoid(-sign * mbuf[...])).astype(jnp.bfloat16)
        if turn == 0:
            loads[1].wait()
            loads[2].wait()

        def grad_body(j, carry):
            cols = pl.ds(pl.multiple_of(j * TILE, TILE), TILE)
            g = jnp.dot(rbuf[...], design[:, cols], preferred_element_type=jnp.float32)
            x = ox[:, cols]
            x = x - eta * (rho * (x - cz[:, cols] + dual[:, cols]) - g)
            ox[:, cols] = x
            if turn == 0:
                nxt = carry + lax.dot_general(
                    x.astype(jnp.bfloat16), design[:, cols], (((1,), (1,)), ((), ())),
                    preferred_element_type=jnp.float32)
            if turn == 1:
                sbuf[:, cols] = x + dual[:, cols]
                half = x.shape[0] // 2
                other = pl.multiple_of((1 - lax.rem(r, 2)) * half, 8)
                _rcopy("rows", sbuf.at[pl.ds(other, half), cols], rows_scr[0].at[:, cols],
                       rows_scr[6].at[j], rows_scr[7].at[j], rpeers[0]).start()
                nxt = carry
            return nxt

        if turn == 0:
            pbuf[...] = lax.fori_loop(0, ntile, grad_body, jnp.zeros(pbuf.shape, jnp.float32))
        else:
            lax.fori_loop(0, ntile, grad_body, 0)

    _rows_allreduce(nx, sbuf, ot, *rows_scr)


def _final_kernel(nr, x, total, dual, prm, ox, oz, ou):
    lim = prm[:, 2:3]
    mean = total[...] / nr
    new_z = mean - jnp.clip(mean, -lim, lim)
    ox[...] = x[...]
    oz[...] = new_z
    ou[...] = dual[...] + x[...] - new_z


def _fused(n_rows, n_feat, design, labels, x0, dual, cz, prm):
    k, width = x0.shape
    s = design.shape[0]
    rblocks = min(k // 8, n_feat)
    rh, cw = k // rblocks, s * rblocks // n_feat
    nx = n_rows // 4
    half, blk = k // 2, k // (2 * nx)
    f32 = jnp.float32
    dma = pltpu.SemaphoreType.DMA
    feat_scr = []
    for _ in range(2):
        feat_scr += [pltpu.VMEM((n_feat, rh, cw), f32), pltpu.VMEM((n_feat, rh, cw), f32)]
        feat_scr += [dma((n_feat,)) for _ in range(4)]
    rows_scr = [
        pltpu.VMEM((half, width), f32),
        pltpu.VMEM((half, width), f32),
        pltpu.VMEM((nx, blk, width), f32),
        pltpu.VMEM((blk, width), f32),
        pltpu.VMEM((nx, blk, width), f32),
        pltpu.VMEM((nx, blk, width), f32),
        dma((QCH,)), dma((QCH,)), dma((QCH, nx)), dma((QCH, nx)), dma((QCH,)), dma((QCH,)),
        dma((QCH, nx)), dma((QCH, nx)), dma((QCH,)), dma((QCH,)),
    ]
    vmem = pl.BlockSpec(memory_space=pltpu.VMEM)
    hbm = pl.BlockSpec(memory_space=pl.ANY)
    out = jax.ShapeDtypeStruct((k, width), f32)
    x, total = pl.pallas_call(
        functools.partial(_fused_kernel, n_feat, n_rows, rh, cw),
        out_shape=(out, out),
        in_specs=[hbm, vmem, vmem, hbm, hbm, vmem],
        out_specs=(vmem, vmem),
        scratch_shapes=[
            pltpu.VMEM((k, s), f32),
            pltpu.VMEM((k, s), f32),
            pltpu.VMEM((k, s), jnp.bfloat16),
            pltpu.VMEM((k, width), f32),
            pltpu.VMEM(design.shape, design.dtype),
            pltpu.VMEM((k, width), f32),
            pltpu.VMEM((k, width), f32),
            dma((3,)),
        ] + feat_scr + rows_scr,
        compiler_params=pltpu.CompilerParams(
            collective_id=0, has_side_effects=True, vmem_limit_bytes=60 * 1024 * 1024),
    )(design, labels, x0, dual, cz, prm)
    tile = pl.BlockSpec((k, 2 * TILE), lambda j: (0, j))
    return pl.pallas_call(
        functools.partial(_final_kernel, n_rows),
        out_shape=(out, out, out),
        grid=(width // (2 * TILE),),
        in_specs=[tile, tile, tile, pl.BlockSpec(prm.shape, lambda j: (0, 0))],
        out_specs=(tile, tile, tile),
    )(x, total, dual, prm)


def per_device(n_rows, n_feat, design, labels, local_x, dual_u, consensus_z, step_size, rho, penalty):
    prm = jnp.stack([step_size, rho, penalty / (rho * n_rows)], axis=1)
    x, new_z, new_u = _fused(n_rows, n_feat, design, labels, local_x[0], dual_u[0],
                             consensus_z, prm)
    return (x[None], new_z, new_u[None])


def solution(mesh):
    in_specs = (
        P("rows", "feat"),
        P(None, "rows"),
        P("rows", None, "feat"),
        P("rows", None, "feat"),
        P(None, "feat"),
        P(),
        P(),
        P(),
    )
    out_specs = (P("rows", None, "feat"), P(None, "feat"), P("rows", None, "feat"))
    fn = functools.partial(per_device, mesh.shape["rows"], mesh.shape["feat"])
    return jax.shard_map(
        fn, mesh=mesh, in_specs=in_specs, out_specs=out_specs, check_vma=False
    )
```

```python
import functools

import jax
import jax.numpy as jnp
from jax import lax
from jax.experimental import pallas as pl
from jax.experimental.pallas import tpu as pltpu
from jax.sharding import PartitionSpec as P

MESH = pl.DeviceIdType.MESH
AXES = ("rows", "feat")
TILE = 1024
QCH = 4


def _device(axis, peer):
    return tuple(peer if a == axis else lax.axis_index(a) for a in AXES)


def _rcopy(axis, src, dst, ss, rs, p):
    return pltpu.make_async_remote_copy(
        src_ref=src, dst_ref=dst, send_sem=ss, recv_sem=rs,
        device_id=_device(axis, p), device_id_type=MESH)


def _feat_allreduce(n, rh, cw, x_ref, o_ref, recv, gath, ss1, rs1, ss2, rs2):
    me = lax.axis_index("feat")
    peers = [lax.rem(me + d, n) for d in range(n)]
    srcs = [lax.rem(me + n - d, n) for d in range(n)]
    cblocks = x_ref.shape[1] // cw

    def block(ref, p):
        r = pl.multiple_of((p // cblocks) * rh, 8)
        c = pl.multiple_of((p % cblocks) * cw, 128)
        return ref.at[pl.ds(r, rh), pl.ds(c, cw)]

    sends = []
    for d in range(1, n):
        c = _rcopy("feat", block(x_ref, peers[d]), recv.at[me], ss1.at[d], rs1.at[d], peers[d])
        c.start()
        sends.append(c)
    acc = block(x_ref, me)[...]
    for d in range(1, n):
        _rcopy("feat", recv.at[srcs[d]], recv.at[srcs[d]], ss1.at[d], rs1.at[d], srcs[d]).wait_recv()
        acc = acc + recv[srcs[d]]
    gath[me] = acc
    sends2 = []
    for d in range(1, n):
        c = _rcopy("feat", gath.at[me], gath.at[me], ss2.at[d], rs2.at[d], peers[d])
        c.start()
        sends2.append(c)
    for c in sends:
        c.wait_send()
    for d in range(1, n):
        _rcopy("feat", gath.at[srcs[d]], gath.at[srcs[d]], ss2.at[d], rs2.at[d], srcs[d]).wait_recv()
    for c in sends2:
        c.wait_send()
    for p in range(n):
        r, c = (p // cblocks) * rh, (p % cblocks) * cw
        o_ref[r:r + rh, c:c + cw] = gath[p]


def _rows_allreduce(nx, x_ref, o_ref, ra, hbuf, rb, rc, gb, ge,
                    ssa, rsa, ssb, rsb, ssc, rsc, ssd, rsd, sse, rse):
    r = lax.axis_index("rows")
    n = 4 * nx
    half, blk = x_ref.shape[0] // 2, x_ref.shape[0] // (2 * nx)
    wq = x_ref.shape[1] // QCH
    c = lax.rem(r, 2)
    xi = lax.rem(r // 2, nx)
    base = r - 2 * xi
    partner = r + 1 - 2 * c
    xpeers = [base + 2 * lax.rem(xi + d, nx) for d in range(nx)]
    xsrcs = [lax.rem(xi + nx - d, nx) for d in range(nx)]
    zpeer = lax.rem(r + 2 * nx, n)
    rcopy = functools.partial(_rcopy, "rows")
    mine = pl.multiple_of(c * half, 8)
    other = pl.multiple_of((1 - c) * half, 8)

    def cols(q):
        return pl.ds(q * wq, wq)

    def rows_of(j):
        return pl.ds(pl.multiple_of(j * blk, 8), blk)

    a = [rcopy(x_ref.at[pl.ds(other, half), cols(q)], ra.at[:, cols(q)], ssa.at[q], rsa.at[q], partner)
         for q in range(QCH)]
    bs = []
    for q in range(QCH):
        a[q].wait()
        hbuf[:, cols(q)] = x_ref[pl.ds(mine, half), cols(q)] + ra[:, cols(q)]
        for d in range(1, nx):
            j = lax.rem(xi + d, nx)
            cp = rcopy(hbuf.at[rows_of(j), cols(q)], rb.at[xi, :, cols(q)],
                       ssb.at[q, d], rsb.at[q, d], xpeers[d])
            cp.start()
            bs.append(cp)
    cz = []
    for q in range(QCH):
        acc = hbuf[rows_of(xi), cols(q)]
        for d in range(1, nx):
            rcopy(rb.at[xsrcs[d], :, cols(q)], rb.at[xsrcs[d], :, cols(q)],
                  ssb.at[q, d], rsb.at[q, d], xpeers[d]).wait_recv()
            acc = acc + rb[xsrcs[d], :, cols(q)]
        gb[xi, :, cols(q)] = acc
        cp = rcopy(gb.at[xi, :, cols(q)], rc.at[:, cols(q)], ssc.at[q], rsc.at[q], zpeer)
        cp.start()
        cz.append(cp)
    ds_ = []
    for q in range(QCH):
        cz[q].wait()
        gb[xi, :, cols(q)] = gb[xi, :, cols(q)] + rc[:, cols(q)]
        for d in range(1, nx):
            cp = rcopy(gb.at[xi, :, cols(q)], gb.at[xi, :, cols(q)], ssd.at[q, d], rsd.at[q, d], xpeers[d])
            cp.start()
            ds_.append(cp)
    e = []
    for q in range(QCH):
        for d in range(1, nx):
            rcopy(gb.at[xsrcs[d], :, cols(q)], gb.at[xsrcs[d], :, cols(q)],
                  ssd.at[q, d], rsd.at[q, d], xpeers[d]).wait_recv()
        cp = rcopy(gb.at[:, :, cols(q)], ge.at[:, :, cols(q)], sse.at[q], rse.at[q], partner)
        cp.start()
        e.append(cp)
    for cp in bs + ds_:
        cp.wait_send()
    for q in range(QCH):
        e[q].wait()
        for j in range(nx):
            o_ref[pl.ds(pl.multiple_of(mine + j * blk, 8), blk), cols(q)] = gb[j, :, cols(q)]
            o_ref[pl.ds(pl.multiple_of(other + j * blk, 8), blk), cols(q)] = ge[j, :, cols(q)]


def _fused_kernel(nf, nr, rh, cw, design_hbm, lab, x0, dual_hbm, cz_hbm, prm,
                  ox, ot, pbuf, mbuf, rbuf, sbuf, design, dual, cz, lsem, *scratch):
    loads = [pltpu.make_async_copy(src, dst, lsem.at[i])
             for i, (src, dst) in enumerate([(design_hbm, design), (dual_hbm, dual), (cz_hbm, cz)])]
    for cp in loads:
        cp.start()
    feat_scr = scratch[:12]
    rows_scr = scratch[12:]
    nx = nr // 4

    me_f = lax.axis_index("feat")
    r = lax.axis_index("rows")
    fpeers = [lax.rem(me_f + d, nf) for d in range(1, nf)]
    c = lax.rem(r, 2)
    xi = lax.rem(r // 2, nx)
    rpeers = [r + 1 - 2 * c, lax.rem(r + 2 * nx, nr)]
    rpeers += [r - 2 * xi + 2 * lax.rem(xi + d, nx) for d in range(1, nx)]

    barrier = pltpu.get_barrier_semaphore()
    for p in fpeers:
        pl.semaphore_signal(barrier, inc=1, device_id=_device("feat", p), device_id_type=MESH)
    for p in rpeers:
        pl.semaphore_signal(barrier, inc=1, device_id=_device("rows", p), device_id_type=MESH)

    eta = prm[:, 0:1]
    rho = prm[:, 1:2]
    ox[...] = x0[...]
    ntile = design.shape[1] // TILE
    loads[0].wait()
    for turn in range(2):
        def margin_body(k, acc):
            cols = pl.ds(pl.multiple_of(k * TILE, TILE), TILE)
            xk = ox[:, cols].astype(jnp.bfloat16)
            return acc + lax.dot_general(
                xk, design[:, cols], (((1,), (1,)), ((), ())),
                preferred_element_type=jnp.float32)

        if turn == 0:
            pbuf[...] = lax.fori_loop(0, ntile, margin_body, jnp.zeros(pbuf.shape, jnp.float32))
        if turn == 0:
            pl.semaphore_wait(barrier, len(fpeers) + len(rpeers))
        _feat_allreduce(nf, rh, cw, pbuf, mbuf, *feat_scr[turn * 6:(turn + 1) * 6])
        sign = lab[...].astype(jnp.float32)
        rbuf[...] = (sign * jax.nn.sigmoid(-sign * mbuf[...])).astype(jnp.bfloat16)
        if turn == 0:
            loads[1].wait()
            loads[2].wait()

        def grad_body(j, carry):
            cols = pl.ds(pl.multiple_of(j * TILE, TILE), TILE)
            g = jnp.dot(rbuf[...], design[:, cols], preferred_element_type=jnp.float32)
            x = ox[:, cols]
            x = x - eta * (rho * (x - cz[:, cols] + dual[:, cols]) - g)
            ox[:, cols] = x
            if turn == 0:
                nxt = carry + lax.dot_general(
                    x.astype(jnp.bfloat16), design[:, cols], (((1,), (1,)), ((), ())),
                    preferred_element_type=jnp.float32)
            if turn == 1:
                sbuf[:, cols] = x + dual[:, cols]
                half = x.shape[0] // 2
                other = pl.multiple_of((1 - lax.rem(r, 2)) * half, 8)
                _rcopy("rows", sbuf.at[pl.ds(other, half), cols], rows_scr[0].at[:, cols],
                       rows_scr[6].at[j], rows_scr[7].at[j], rpeers[0]).start()
                nxt = carry
            return nxt

        if turn == 0:
            pbuf[...] = lax.fori_loop(0, ntile, grad_body, jnp.zeros(pbuf.shape, jnp.float32))
        else:
            lax.fori_loop(0, ntile, grad_body, 0)

    _rows_allreduce(nx, sbuf, ot, *rows_scr)


def _final_kernel(nr, x, total, dual, prm, ox, oz, ou):
    lim = prm[:, 2:3]
    mean = total[...] / nr
    new_z = mean - jnp.clip(mean, -lim, lim)
    ox[...] = x[...]
    oz[...] = new_z
    ou[...] = dual[...] + x[...] - new_z


def _fused(n_rows, n_feat, design, labels, x0, dual, cz, prm):
    k, width = x0.shape
    s = design.shape[0]
    rblocks = min(k // 8, n_feat)
    rh, cw = k // rblocks, s * rblocks // n_feat
    nx = n_rows // 4
    half, blk = k // 2, k // (2 * nx)
    f32 = jnp.float32
    dma = pltpu.SemaphoreType.DMA
    feat_scr = []
    for _ in range(2):
        feat_scr += [pltpu.VMEM((n_feat, rh, cw), f32), pltpu.VMEM((n_feat, rh, cw), f32)]
        feat_scr += [dma((n_feat,)) for _ in range(4)]
    rows_scr = [
        pltpu.VMEM((half, width), f32),
        pltpu.VMEM((half, width), f32),
        pltpu.VMEM((nx, blk, width), f32),
        pltpu.VMEM((blk, width), f32),
        pltpu.VMEM((nx, blk, width), f32),
        pltpu.VMEM((nx, blk, width), f32),
        dma((QCH,)), dma((QCH,)), dma((QCH, nx)), dma((QCH, nx)), dma((QCH,)), dma((QCH,)),
        dma((QCH, nx)), dma((QCH, nx)), dma((QCH,)), dma((QCH,)),
    ]
    vmem = pl.BlockSpec(memory_space=pltpu.VMEM)
    hbm = pl.BlockSpec(memory_space=pl.ANY)
    out = jax.ShapeDtypeStruct((k, width), f32)
    x, total = pl.pallas_call(
        functools.partial(_fused_kernel, n_feat, n_rows, rh, cw),
        out_shape=(out, out),
        in_specs=[hbm, vmem, vmem, hbm, hbm, vmem],
        out_specs=(vmem, vmem),
        scratch_shapes=[
            pltpu.VMEM((k, s), f32),
            pltpu.VMEM((k, s), f32),
            pltpu.VMEM((k, s), jnp.bfloat16),
            pltpu.VMEM((k, width), f32),
            pltpu.VMEM(design.shape, design.dtype),
            pltpu.VMEM((k, width), f32),
            pltpu.VMEM((k, width), f32),
            dma((3,)),
        ] + feat_scr + rows_scr,
        compiler_params=pltpu.CompilerParams(
            collective_id=0, has_side_effects=True, vmem_limit_bytes=60 * 1024 * 1024),
    )(design, labels, x0, dual, cz, prm)
    tile = pl.BlockSpec((k, 2 * TILE), lambda j: (0, j))
    return pl.pallas_call(
        functools.partial(_final_kernel, n_rows),
        out_shape=(out, out, out),
        grid=(width // (2 * TILE),),
        in_specs=[tile, tile, tile, pl.BlockSpec(prm.shape, lambda j: (0, 0))],
        out_specs=(tile, tile, tile),
    )(x, total, dual, prm)


def per_device(n_rows, n_feat, design, labels, local_x, dual_u, consensus_z, step_size, rho, penalty):
    prm = jnp.stack([step_size, rho, penalty / (rho * n_rows)], axis=1)
    x, new_z, new_u = _fused(n_rows, n_feat, design, labels, local_x[0], dual_u[0],
                             consensus_z, prm)
    return (x[None], new_z, new_u[None])


def solution(mesh):
    in_specs = (
        P("rows", "feat"),
        P(None, "rows"),
        P("rows", None, "feat"),
        P("rows", None, "feat"),
        P(None, "feat"),
        P(),
        P(),
        P(),
    )
    out_specs = (P("rows", None, "feat"), P(None, "feat"), P("rows", None, "feat"))
    fn = functools.partial(per_device, mesh.shape["rows"], mesh.shape["feat"])
    return jax.shard_map(
        fn, mesh=mesh, in_specs=in_specs, out_specs=out_specs, check_vma=False
    )
```

```python
import functools

import jax
import jax.numpy as jnp
from jax import lax
from jax.experimental import pallas as pl
from jax.experimental.pallas import tpu as pltpu
from jax.sharding import PartitionSpec as P

MESH = pl.DeviceIdType.MESH
AXES = ("rows", "feat")
TILE = 1024
QCH = 4


def _device(axis, peer):
    return tuple(peer if a == axis else lax.axis_index(a) for a in AXES)


def _rcopy(axis, src, dst, ss, rs, p):
    return pltpu.make_async_remote_copy(
        src_ref=src, dst_ref=dst, send_sem=ss, recv_sem=rs,
        device_id=_device(axis, p), device_id_type=MESH)


def _feat_allreduce(n, rh, cw, x_ref, o_ref, recv, gath, ss1, rs1, ss2, rs2):
    me = lax.axis_index("feat")
    peers = [lax.rem(me + d, n) for d in range(n)]
    srcs = [lax.rem(me + n - d, n) for d in range(n)]
    cblocks = x_ref.shape[1] // cw

    def block(ref, p):
        r = pl.multiple_of((p // cblocks) * rh, 8)
        c = pl.multiple_of((p % cblocks) * cw, 128)
        return ref.at[pl.ds(r, rh), pl.ds(c, cw)]

    sends = []
    for d in range(1, n):
        c = _rcopy("feat", block(x_ref, peers[d]), recv.at[me], ss1.at[d], rs1.at[d], peers[d])
        c.start()
        sends.append(c)
    acc = block(x_ref, me)[...]
    for d in range(1, n):
        _rcopy("feat", recv.at[srcs[d]], recv.at[srcs[d]], ss1.at[d], rs1.at[d], srcs[d]).wait_recv()
        acc = acc + recv[srcs[d]]
    gath[me] = acc
    sends2 = []
    for d in range(1, n):
        c = _rcopy("feat", gath.at[me], gath.at[me], ss2.at[d], rs2.at[d], peers[d])
        c.start()
        sends2.append(c)
    for c in sends:
        c.wait_send()
    for d in range(1, n):
        _rcopy("feat", gath.at[srcs[d]], gath.at[srcs[d]], ss2.at[d], rs2.at[d], srcs[d]).wait_recv()
    for c in sends2:
        c.wait_send()
    for p in range(n):
        r, c = (p // cblocks) * rh, (p % cblocks) * cw
        o_ref[r:r + rh, c:c + cw] = gath[p]


def _rows_allreduce(nx, x_ref, o_ref, ra, hbuf, rb, rc, gb, ge,
                    ssa, rsa, ssb, rsb, ssc, rsc, ssd, rsd, sse, rse):
    r = lax.axis_index("rows")
    n = 4 * nx
    half, blk = x_ref.shape[0] // 2, x_ref.shape[0] // (2 * nx)
    wq = x_ref.shape[1] // QCH
    c = lax.rem(r, 2)
    xi = lax.rem(r // 2, nx)
    base = r - 2 * xi
    partner = r + 1 - 2 * c
    xpeers = [base + 2 * lax.rem(xi + d, nx) for d in range(nx)]
    xsrcs = [lax.rem(xi + nx - d, nx) for d in range(nx)]
    zpeer = lax.rem(r + 2 * nx, n)
    rcopy = functools.partial(_rcopy, "rows")
    mine = pl.multiple_of(c * half, 8)
    other = pl.multiple_of((1 - c) * half, 8)

    def cols(q):
        return pl.ds(q * wq, wq)

    def rows_of(j):
        return pl.ds(pl.multiple_of(j * blk, 8), blk)

    a = [rcopy(x_ref.at[pl.ds(other, half), cols(q)], ra.at[:, cols(q)], ssa.at[q], rsa.at[q], partner)
         for q in range(QCH)]
    bs = []
    for q in range(QCH):
        a[q].wait()
        hbuf[:, cols(q)] = x_ref[pl.ds(mine, half), cols(q)] + ra[:, cols(q)]
        for d in range(1, nx):
            j = lax.rem(xi + d, nx)
            cp = rcopy(hbuf.at[rows_of(j), cols(q)], rb.at[xi, :, cols(q)],
                       ssb.at[q, d], rsb.at[q, d], xpeers[d])
            cp.start()
            bs.append(cp)
    cz = []
    for q in range(QCH):
        acc = hbuf[rows_of(xi), cols(q)]
        for d in range(1, nx):
            rcopy(rb.at[xsrcs[d], :, cols(q)], rb.at[xsrcs[d], :, cols(q)],
                  ssb.at[q, d], rsb.at[q, d], xpeers[d]).wait_recv()
            acc = acc + rb[xsrcs[d], :, cols(q)]
        gb[xi, :, cols(q)] = acc
        cp = rcopy(gb.at[xi, :, cols(q)], rc.at[:, cols(q)], ssc.at[q], rsc.at[q], zpeer)
        cp.start()
        cz.append(cp)
    ds_ = []
    for q in range(QCH):
        cz[q].wait()
        gb[xi, :, cols(q)] = gb[xi, :, cols(q)] + rc[:, cols(q)]
        for d in range(1, nx):
            cp = rcopy(gb.at[xi, :, cols(q)], gb.at[xi, :, cols(q)], ssd.at[q, d], rsd.at[q, d], xpeers[d])
            cp.start()
            ds_.append(cp)
    e = []
    for q in range(QCH):
        for d in range(1, nx):
            rcopy(gb.at[xsrcs[d], :, cols(q)], gb.at[xsrcs[d], :, cols(q)],
                  ssd.at[q, d], rsd.at[q, d], xpeers[d]).wait_recv()
        cp = rcopy(gb.at[:, :, cols(q)], ge.at[:, :, cols(q)], sse.at[q], rse.at[q], partner)
        cp.start()
        e.append(cp)
    for cp in bs + ds_:
        cp.wait_send()
    for q in range(QCH):
        e[q].wait()
        for j in range(nx):
            o_ref[pl.ds(pl.multiple_of(mine + j * blk, 8), blk), cols(q)] = gb[j, :, cols(q)]
            o_ref[pl.ds(pl.multiple_of(other + j * blk, 8), blk), cols(q)] = ge[j, :, cols(q)]


def _fused_kernel(nf, nr, rh, cw, design_hbm, lab, x0, dual_hbm, cz_hbm, prm,
                  ox, ot, pbuf, mbuf, rbuf, sbuf, design, dual, cz, lsem, *scratch):
    loads = [pltpu.make_async_copy(src, dst, lsem.at[i])
             for i, (src, dst) in enumerate([(design_hbm, design), (dual_hbm, dual), (cz_hbm, cz)])]
    for cp in loads:
        cp.start()
    feat_scr = scratch[:12]
    rows_scr = scratch[12:]
    nx = nr // 4

    me_f = lax.axis_index("feat")
    r = lax.axis_index("rows")
    fpeers = [lax.rem(me_f + d, nf) for d in range(1, nf)]
    c = lax.rem(r, 2)
    xi = lax.rem(r // 2, nx)
    rpeers = [r + 1 - 2 * c, lax.rem(r + 2 * nx, nr)]
    rpeers += [r - 2 * xi + 2 * lax.rem(xi + d, nx) for d in range(1, nx)]

    barrier = pltpu.get_barrier_semaphore()
    for p in fpeers:
        pl.semaphore_signal(barrier, inc=1, device_id=_device("feat", p), device_id_type=MESH)
    for p in rpeers:
        pl.semaphore_signal(barrier, inc=1, device_id=_device("rows", p), device_id_type=MESH)

    eta = prm[:, 0:1]
    rho = prm[:, 1:2]
    ox[...] = x0[...]
    ntile = design.shape[1] // TILE
    loads[0].wait()
    for turn in range(2):
        def margin_body(k, acc):
            cols = pl.ds(pl.multiple_of(k * TILE, TILE), TILE)
            xk = ox[:, cols].astype(jnp.bfloat16)
            return acc + lax.dot_general(
                xk, design[:, cols], (((1,), (1,)), ((), ())),
                preferred_element_type=jnp.float32)

        if turn == 0:
            pbuf[...] = lax.fori_loop(0, ntile, margin_body, jnp.zeros(pbuf.shape, jnp.float32))
        if turn == 0:
            pl.semaphore_wait(barrier, len(fpeers) + len(rpeers))
        _feat_allreduce(nf, rh, cw, pbuf, mbuf, *feat_scr[turn * 6:(turn + 1) * 6])
        sign = lab[...].astype(jnp.float32)
        rbuf[...] = (sign * jax.nn.sigmoid(-sign * mbuf[...])).astype(jnp.bfloat16)
        if turn == 0:
            loads[1].wait()
            loads[2].wait()

        def grad_body(j, carry):
            cols = pl.ds(pl.multiple_of(j * TILE, TILE), TILE)
            g = jnp.dot(rbuf[...], design[:, cols], preferred_element_type=jnp.float32)
            x = ox[:, cols]
            x = x - eta * (rho * (x - cz[:, cols] + dual[:, cols]) - g)
            ox[:, cols] = x
            if turn == 0:
                nxt = carry + lax.dot_general(
                    x.astype(jnp.bfloat16), design[:, cols], (((1,), (1,)), ((), ())),
                    preferred_element_type=jnp.float32)
            if turn == 1:
                sbuf[:, cols] = x + dual[:, cols]
                half = x.shape[0] // 2
                other = pl.multiple_of((1 - lax.rem(r, 2)) * half, 8)
                _rcopy("rows", sbuf.at[pl.ds(other, half), cols], rows_scr[0].at[:, cols],
                       rows_scr[6].at[j], rows_scr[7].at[j], rpeers[0]).start()
                nxt = carry
            return nxt

        if turn == 0:
            pbuf[...] = lax.fori_loop(0, ntile, grad_body, jnp.zeros(pbuf.shape, jnp.float32))
        else:
            lax.fori_loop(0, ntile, grad_body, 0)

    _rows_allreduce(nx, sbuf, ot, *rows_scr)


def _final_kernel(nr, x, total, dual, prm, ox, oz, ou):
    lim = prm[:, 2:3]
    mean = total[...] / nr
    new_z = mean - jnp.clip(mean, -lim, lim)
    ox[...] = x[...]
    oz[...] = new_z
    ou[...] = dual[...] + x[...] - new_z


def _fused(n_rows, n_feat, design, labels, x0, dual, cz, prm):
    k, width = x0.shape
    s = design.shape[0]
    rblocks = min(k // 8, n_feat)
    rh, cw = k // rblocks, s * rblocks // n_feat
    nx = n_rows // 4
    half, blk = k // 2, k // (2 * nx)
    f32 = jnp.float32
    dma = pltpu.SemaphoreType.DMA
    feat_scr = []
    for _ in range(2):
        feat_scr += [pltpu.VMEM((n_feat, rh, cw), f32), pltpu.VMEM((n_feat, rh, cw), f32)]
        feat_scr += [dma((n_feat,)) for _ in range(4)]
    rows_scr = [
        pltpu.VMEM((half, width), f32),
        pltpu.VMEM((half, width), f32),
        pltpu.VMEM((nx, blk, width), f32),
        pltpu.VMEM((blk, width), f32),
        pltpu.VMEM((nx, blk, width), f32),
        pltpu.VMEM((nx, blk, width), f32),
        dma((QCH,)), dma((QCH,)), dma((QCH, nx)), dma((QCH, nx)), dma((QCH,)), dma((QCH,)),
        dma((QCH, nx)), dma((QCH, nx)), dma((QCH,)), dma((QCH,)),
    ]
    vmem = pl.BlockSpec(memory_space=pltpu.VMEM)
    hbm = pl.BlockSpec(memory_space=pl.ANY)
    out = jax.ShapeDtypeStruct((k, width), f32)
    x, total = pl.pallas_call(
        functools.partial(_fused_kernel, n_feat, n_rows, rh, cw),
        out_shape=(out, out),
        in_specs=[hbm, vmem, vmem, hbm, hbm, vmem],
        out_specs=(vmem, vmem),
        scratch_shapes=[
            pltpu.VMEM((k, s), f32),
            pltpu.VMEM((k, s), f32),
            pltpu.VMEM((k, s), jnp.bfloat16),
            pltpu.VMEM((k, width), f32),
            pltpu.VMEM(design.shape, design.dtype),
            pltpu.VMEM((k, width), f32),
            pltpu.VMEM((k, width), f32),
            dma((3,)),
        ] + feat_scr + rows_scr,
        compiler_params=pltpu.CompilerParams(
            collective_id=0, has_side_effects=True, vmem_limit_bytes=60 * 1024 * 1024),
    )(design, labels, x0, dual, cz, prm)
    tile = pl.BlockSpec((k, 1024), lambda j: (0, j))
    return pl.pallas_call(
        functools.partial(_final_kernel, n_rows),
        out_shape=(out, out, out),
        grid=(width // (1024),),
        in_specs=[tile, tile, tile, pl.BlockSpec(prm.shape, lambda j: (0, 0))],
        out_specs=(tile, tile, tile),
    )(x, total, dual, prm)


def per_device(n_rows, n_feat, design, labels, local_x, dual_u, consensus_z, step_size, rho, penalty):
    prm = jnp.stack([step_size, rho, penalty / (rho * n_rows)], axis=1)
    x, new_z, new_u = _fused(n_rows, n_feat, design, labels, local_x[0], dual_u[0],
                             consensus_z, prm)
    return (x[None], new_z, new_u[None])


def solution(mesh):
    in_specs = (
        P("rows", "feat"),
        P(None, "rows"),
        P("rows", None, "feat"),
        P("rows", None, "feat"),
        P(None, "feat"),
        P(),
        P(),
        P(),
    )
    out_specs = (P("rows", None, "feat"), P(None, "feat"), P("rows", None, "feat"))
    fn = functools.partial(per_device, mesh.shape["rows"], mesh.shape["feat"])
    return jax.shard_map(
        fn, mesh=mesh, in_specs=in_specs, out_specs=out_specs, check_vma=False
    )
```

```python
import functools

import jax
import jax.numpy as jnp
from jax import lax
from jax.experimental import pallas as pl
from jax.experimental.pallas import tpu as pltpu
from jax.sharding import PartitionSpec as P

MESH = pl.DeviceIdType.MESH
AXES = ("rows", "feat")
TILE = 1024
QCH = 4


def _device(axis, peer):
    return tuple(peer if a == axis else lax.axis_index(a) for a in AXES)


def _rcopy(axis, src, dst, ss, rs, p):
    return pltpu.make_async_remote_copy(
        src_ref=src, dst_ref=dst, send_sem=ss, recv_sem=rs,
        device_id=_device(axis, p), device_id_type=MESH)


def _feat_allreduce(n, rh, cw, x_ref, o_ref, recv, gath, ss1, rs1, ss2, rs2):
    me = lax.axis_index("feat")
    peers = [lax.rem(me + d, n) for d in range(n)]
    srcs = [lax.rem(me + n - d, n) for d in range(n)]
    cblocks = x_ref.shape[1] // cw

    def block(ref, p):
        r = pl.multiple_of((p // cblocks) * rh, 8)
        c = pl.multiple_of((p % cblocks) * cw, 128)
        return ref.at[pl.ds(r, rh), pl.ds(c, cw)]

    sends = []
    for d in range(1, n):
        c = _rcopy("feat", block(x_ref, peers[d]), recv.at[me], ss1.at[d], rs1.at[d], peers[d])
        c.start()
        sends.append(c)
    acc = block(x_ref, me)[...]
    for d in range(1, n):
        _rcopy("feat", recv.at[srcs[d]], recv.at[srcs[d]], ss1.at[d], rs1.at[d], srcs[d]).wait_recv()
        acc = acc + recv[srcs[d]]
    gath[me] = acc
    sends2 = []
    for d in range(1, n):
        c = _rcopy("feat", gath.at[me], gath.at[me], ss2.at[d], rs2.at[d], peers[d])
        c.start()
        sends2.append(c)
    for c in sends:
        c.wait_send()
    for d in range(1, n):
        _rcopy("feat", gath.at[srcs[d]], gath.at[srcs[d]], ss2.at[d], rs2.at[d], srcs[d]).wait_recv()
    for c in sends2:
        c.wait_send()
    for p in range(n):
        r, c = (p // cblocks) * rh, (p % cblocks) * cw
        o_ref[r:r + rh, c:c + cw] = gath[p]


def _rows_allreduce(nx, x_ref, o_ref, ra, hbuf, rb, rc, gb, ge,
                    ssa, rsa, ssb, rsb, ssc, rsc, ssd, rsd, sse, rse):
    r = lax.axis_index("rows")
    n = 4 * nx
    half, blk = x_ref.shape[0] // 2, x_ref.shape[0] // (2 * nx)
    wq = x_ref.shape[1] // QCH
    c = lax.rem(r, 2)
    xi = lax.rem(r // 2, nx)
    base = r - 2 * xi
    partner = r + 1 - 2 * c
    xpeers = [base + 2 * lax.rem(xi + d, nx) for d in range(nx)]
    xsrcs = [lax.rem(xi + nx - d, nx) for d in range(nx)]
    zpeer = lax.rem(r + 2 * nx, n)
    rcopy = functools.partial(_rcopy, "rows")
    mine = pl.multiple_of(c * half, 8)
    other = pl.multiple_of((1 - c) * half, 8)

    def cols(q):
        return pl.ds(q * wq, wq)

    def rows_of(j):
        return pl.ds(pl.multiple_of(j * blk, 8), blk)

    a = [rcopy(x_ref.at[pl.ds(other, half), cols(q)], ra.at[:, cols(q)], ssa.at[q], rsa.at[q], partner)
         for q in range(QCH)]
    bs = []
    for q in range(QCH):
        a[q].wait()
        hbuf[:, cols(q)] = x_ref[pl.ds(mine, half), cols(q)] + ra[:, cols(q)]
        for d in range(1, nx):
            j = lax.rem(xi + d, nx)
            cp = rcopy(hbuf.at[rows_of(j), cols(q)], rb.at[xi, :, cols(q)],
                       ssb.at[q, d], rsb.at[q, d], xpeers[d])
            cp.start()
            bs.append(cp)
    cz = []
    for q in range(QCH):
        acc = hbuf[rows_of(xi), cols(q)]
        for d in range(1, nx):
            rcopy(rb.at[xsrcs[d], :, cols(q)], rb.at[xsrcs[d], :, cols(q)],
                  ssb.at[q, d], rsb.at[q, d], xpeers[d]).wait_recv()
            acc = acc + rb[xsrcs[d], :, cols(q)]
        gb[xi, :, cols(q)] = acc
        cp = rcopy(gb.at[xi, :, cols(q)], rc.at[:, cols(q)], ssc.at[q], rsc.at[q], zpeer)
        cp.start()
        cz.append(cp)
    ds_ = []
    for q in range(QCH):
        cz[q].wait()
        gb[xi, :, cols(q)] = gb[xi, :, cols(q)] + rc[:, cols(q)]
        for d in range(1, nx):
            cp = rcopy(gb.at[xi, :, cols(q)], gb.at[xi, :, cols(q)], ssd.at[q, d], rsd.at[q, d], xpeers[d])
            cp.start()
            ds_.append(cp)
    e = []
    for q in range(QCH):
        for d in range(1, nx):
            rcopy(gb.at[xsrcs[d], :, cols(q)], gb.at[xsrcs[d], :, cols(q)],
                  ssd.at[q, d], rsd.at[q, d], xpeers[d]).wait_recv()
        cp = rcopy(gb.at[:, :, cols(q)], ge.at[:, :, cols(q)], sse.at[q], rse.at[q], partner)
        cp.start()
        e.append(cp)
    for cp in bs + ds_:
        cp.wait_send()
    for q in range(QCH):
        e[q].wait()
        for j in range(nx):
            o_ref[pl.ds(pl.multiple_of(mine + j * blk, 8), blk), cols(q)] = gb[j, :, cols(q)]
            o_ref[pl.ds(pl.multiple_of(other + j * blk, 8), blk), cols(q)] = ge[j, :, cols(q)]


def _fused_kernel(nf, nr, rh, cw, design_hbm, lab, x0, dual_hbm, cz_hbm, prm,
                  ox, ot, pbuf, mbuf, rbuf, sbuf, design, dual, cz, lsem, *scratch):
    loads = [pltpu.make_async_copy(src, dst, lsem.at[i])
             for i, (src, dst) in enumerate([(design_hbm, design), (dual_hbm, dual), (cz_hbm, cz)])]
    for cp in loads:
        cp.start()
    feat_scr = scratch[:12]
    rows_scr = scratch[12:]
    nx = nr // 4

    me_f = lax.axis_index("feat")
    r = lax.axis_index("rows")
    fpeers = [lax.rem(me_f + d, nf) for d in range(1, nf)]
    c = lax.rem(r, 2)
    xi = lax.rem(r // 2, nx)
    rpeers = [r + 1 - 2 * c, lax.rem(r + 2 * nx, nr)]
    rpeers += [r - 2 * xi + 2 * lax.rem(xi + d, nx) for d in range(1, nx)]

    barrier = pltpu.get_barrier_semaphore()
    for p in fpeers:
        pl.semaphore_signal(barrier, inc=1, device_id=_device("feat", p), device_id_type=MESH)
    for p in rpeers:
        pl.semaphore_signal(barrier, inc=1, device_id=_device("rows", p), device_id_type=MESH)

    eta = prm[:, 0:1]
    rho = prm[:, 1:2]
    ox[...] = x0[...]
    ntile = design.shape[1] // TILE
    loads[0].wait()
    for turn in range(2):
        def margin_body(k, acc):
            cols = pl.ds(pl.multiple_of(k * TILE, TILE), TILE)
            xk = ox[:, cols].astype(jnp.bfloat16)
            return acc + lax.dot_general(
                xk, design[:, cols], (((1,), (1,)), ((), ())),
                preferred_element_type=jnp.float32)

        if turn == 0:
            pbuf[...] = lax.fori_loop(0, ntile, margin_body, jnp.zeros(pbuf.shape, jnp.float32), unroll=True)
        if turn == 0:
            pl.semaphore_wait(barrier, len(fpeers) + len(rpeers))
        _feat_allreduce(nf, rh, cw, pbuf, mbuf, *feat_scr[turn * 6:(turn + 1) * 6])
        sign = lab[...].astype(jnp.float32)
        rbuf[...] = (sign * jax.nn.sigmoid(-sign * mbuf[...])).astype(jnp.bfloat16)
        if turn == 0:
            loads[1].wait()
            loads[2].wait()

        def grad_body(j, carry):
            cols = pl.ds(pl.multiple_of(j * TILE, TILE), TILE)
            g = jnp.dot(rbuf[...], design[:, cols], preferred_element_type=jnp.float32)
            x = ox[:, cols]
            x = x - eta * (rho * (x - cz[:, cols] + dual[:, cols]) - g)
            ox[:, cols] = x
            if turn == 0:
                nxt = carry + lax.dot_general(
                    x.astype(jnp.bfloat16), design[:, cols], (((1,), (1,)), ((), ())),
                    preferred_element_type=jnp.float32)
            if turn == 1:
                sbuf[:, cols] = x + dual[:, cols]
                half = x.shape[0] // 2
                other = pl.multiple_of((1 - lax.rem(r, 2)) * half, 8)
                _rcopy("rows", sbuf.at[pl.ds(other, half), cols], rows_scr[0].at[:, cols],
                       rows_scr[6].at[j], rows_scr[7].at[j], rpeers[0]).start()
                nxt = carry
            return nxt

        if turn == 0:
            pbuf[...] = lax.fori_loop(0, ntile, grad_body, jnp.zeros(pbuf.shape, jnp.float32), unroll=True)
        else:
            lax.fori_loop(0, ntile, grad_body, 0, unroll=True)

    _rows_allreduce(nx, sbuf, ot, *rows_scr)


def _final_kernel(nr, x, total, dual, prm, ox, oz, ou):
    lim = prm[:, 2:3]
    mean = total[...] / nr
    new_z = mean - jnp.clip(mean, -lim, lim)
    ox[...] = x[...]
    oz[...] = new_z
    ou[...] = dual[...] + x[...] - new_z


def _fused(n_rows, n_feat, design, labels, x0, dual, cz, prm):
    k, width = x0.shape
    s = design.shape[0]
    rblocks = min(k // 8, n_feat)
    rh, cw = k // rblocks, s * rblocks // n_feat
    nx = n_rows // 4
    half, blk = k // 2, k // (2 * nx)
    f32 = jnp.float32
    dma = pltpu.SemaphoreType.DMA
    feat_scr = []
    for _ in range(2):
        feat_scr += [pltpu.VMEM((n_feat, rh, cw), f32), pltpu.VMEM((n_feat, rh, cw), f32)]
        feat_scr += [dma((n_feat,)) for _ in range(4)]
    rows_scr = [
        pltpu.VMEM((half, width), f32),
        pltpu.VMEM((half, width), f32),
        pltpu.VMEM((nx, blk, width), f32),
        pltpu.VMEM((blk, width), f32),
        pltpu.VMEM((nx, blk, width), f32),
        pltpu.VMEM((nx, blk, width), f32),
        dma((QCH,)), dma((QCH,)), dma((QCH, nx)), dma((QCH, nx)), dma((QCH,)), dma((QCH,)),
        dma((QCH, nx)), dma((QCH, nx)), dma((QCH,)), dma((QCH,)),
    ]
    vmem = pl.BlockSpec(memory_space=pltpu.VMEM)
    hbm = pl.BlockSpec(memory_space=pl.ANY)
    out = jax.ShapeDtypeStruct((k, width), f32)
    x, total = pl.pallas_call(
        functools.partial(_fused_kernel, n_feat, n_rows, rh, cw),
        out_shape=(out, out),
        in_specs=[hbm, vmem, vmem, hbm, hbm, vmem],
        out_specs=(vmem, vmem),
        scratch_shapes=[
            pltpu.VMEM((k, s), f32),
            pltpu.VMEM((k, s), f32),
            pltpu.VMEM((k, s), jnp.bfloat16),
            pltpu.VMEM((k, width), f32),
            pltpu.VMEM(design.shape, design.dtype),
            pltpu.VMEM((k, width), f32),
            pltpu.VMEM((k, width), f32),
            dma((3,)),
        ] + feat_scr + rows_scr,
        compiler_params=pltpu.CompilerParams(
            collective_id=0, has_side_effects=True, vmem_limit_bytes=60 * 1024 * 1024),
    )(design, labels, x0, dual, cz, prm)
    tile = pl.BlockSpec((k, 2 * TILE), lambda j: (0, j))
    return pl.pallas_call(
        functools.partial(_final_kernel, n_rows),
        out_shape=(out, out, out),
        grid=(width // (2 * TILE),),
        in_specs=[tile, tile, tile, pl.BlockSpec(prm.shape, lambda j: (0, 0))],
        out_specs=(tile, tile, tile),
    )(x, total, dual, prm)


def per_device(n_rows, n_feat, design, labels, local_x, dual_u, consensus_z, step_size, rho, penalty):
    prm = jnp.stack([step_size, rho, penalty / (rho * n_rows)], axis=1)
    x, new_z, new_u = _fused(n_rows, n_feat, design, labels, local_x[0], dual_u[0],
                             consensus_z, prm)
    return (x[None], new_z, new_u[None])


def solution(mesh):
    in_specs = (
        P("rows", "feat"),
        P(None, "rows"),
        P("rows", None, "feat"),
        P("rows", None, "feat"),
        P(None, "feat"),
        P(),
        P(),
        P(),
    )
    out_specs = (P("rows", None, "feat"), P(None, "feat"), P("rows", None, "feat"))
    fn = functools.partial(per_device, mesh.shape["rows"], mesh.shape["feat"])
    return jax.shard_map(
        fn, mesh=mesh, in_specs=in_specs, out_specs=out_specs, check_vma=False
    )
```

```python
import functools

import jax
import jax.numpy as jnp
from jax import lax
from jax.experimental import pallas as pl
from jax.experimental.pallas import tpu as pltpu
from jax.sharding import PartitionSpec as P

MESH = pl.DeviceIdType.MESH
AXES = ("rows", "feat")
TILE = 1024
QCH = 8


def _device(axis, peer):
    return tuple(peer if a == axis else lax.axis_index(a) for a in AXES)


def _rcopy(axis, src, dst, ss, rs, p):
    return pltpu.make_async_remote_copy(
        src_ref=src, dst_ref=dst, send_sem=ss, recv_sem=rs,
        device_id=_device(axis, p), device_id_type=MESH)


def _feat_allreduce(n, rh, cw, x_ref, o_ref, recv, gath, ss1, rs1, ss2, rs2):
    me = lax.axis_index("feat")
    peers = [lax.rem(me + d, n) for d in range(n)]
    srcs = [lax.rem(me + n - d, n) for d in range(n)]
    cblocks = x_ref.shape[1] // cw

    def block(ref, p):
        r = pl.multiple_of((p // cblocks) * rh, 8)
        c = pl.multiple_of((p % cblocks) * cw, 128)
        return ref.at[pl.ds(r, rh), pl.ds(c, cw)]

    sends = []
    for d in range(1, n):
        c = _rcopy("feat", block(x_ref, peers[d]), recv.at[me], ss1.at[d], rs1.at[d], peers[d])
        c.start()
        sends.append(c)
    acc = block(x_ref, me)[...]
    for d in range(1, n):
        _rcopy("feat", recv.at[srcs[d]], recv.at[srcs[d]], ss1.at[d], rs1.at[d], srcs[d]).wait_recv()
        acc = acc + recv[srcs[d]]
    gath[me] = acc
    sends2 = []
    for d in range(1, n):
        c = _rcopy("feat", gath.at[me], gath.at[me], ss2.at[d], rs2.at[d], peers[d])
        c.start()
        sends2.append(c)
    for c in sends:
        c.wait_send()
    for d in range(1, n):
        _rcopy("feat", gath.at[srcs[d]], gath.at[srcs[d]], ss2.at[d], rs2.at[d], srcs[d]).wait_recv()
    for c in sends2:
        c.wait_send()
    for p in range(n):
        r, c = (p // cblocks) * rh, (p % cblocks) * cw
        o_ref[r:r + rh, c:c + cw] = gath[p]


def _rows_allreduce(nx, x_ref, o_ref, ra, hbuf, rb, rc, gb, ge,
                    ssa, rsa, ssb, rsb, ssc, rsc, ssd, rsd, sse, rse):
    r = lax.axis_index("rows")
    n = 4 * nx
    half, blk = x_ref.shape[0] // 2, x_ref.shape[0] // (2 * nx)
    wq = x_ref.shape[1] // QCH
    c = lax.rem(r, 2)
    xi = lax.rem(r // 2, nx)
    base = r - 2 * xi
    partner = r + 1 - 2 * c
    xpeers = [base + 2 * lax.rem(xi + d, nx) for d in range(nx)]
    xsrcs = [lax.rem(xi + nx - d, nx) for d in range(nx)]
    zpeer = lax.rem(r + 2 * nx, n)
    rcopy = functools.partial(_rcopy, "rows")
    mine = pl.multiple_of(c * half, 8)
    other = pl.multiple_of((1 - c) * half, 8)

    def cols(q):
        return pl.ds(q * wq, wq)

    def rows_of(j):
        return pl.ds(pl.multiple_of(j * blk, 8), blk)

    a = [rcopy(x_ref.at[pl.ds(other, half), cols(q)], ra.at[:, cols(q)], ssa.at[q], rsa.at[q], partner)
         for q in range(QCH)]
    bs = []
    for q in range(QCH):
        a[q].wait()
        hbuf[:, cols(q)] = x_ref[pl.ds(mine, half), cols(q)] + ra[:, cols(q)]
        for d in range(1, nx):
            j = lax.rem(xi + d, nx)
            cp = rcopy(hbuf.at[rows_of(j), cols(q)], rb.at[xi, :, cols(q)],
                       ssb.at[q, d], rsb.at[q, d], xpeers[d])
            cp.start()
            bs.append(cp)
    cz = []
    for q in range(QCH):
        acc = hbuf[rows_of(xi), cols(q)]
        for d in range(1, nx):
            rcopy(rb.at[xsrcs[d], :, cols(q)], rb.at[xsrcs[d], :, cols(q)],
                  ssb.at[q, d], rsb.at[q, d], xpeers[d]).wait_recv()
            acc = acc + rb[xsrcs[d], :, cols(q)]
        gb[xi, :, cols(q)] = acc
        cp = rcopy(gb.at[xi, :, cols(q)], rc.at[:, cols(q)], ssc.at[q], rsc.at[q], zpeer)
        cp.start()
        cz.append(cp)
    ds_ = []
    for q in range(QCH):
        cz[q].wait()
        gb[xi, :, cols(q)] = gb[xi, :, cols(q)] + rc[:, cols(q)]
        for d in range(1, nx):
            cp = rcopy(gb.at[xi, :, cols(q)], gb.at[xi, :, cols(q)], ssd.at[q, d], rsd.at[q, d], xpeers[d])
            cp.start()
            ds_.append(cp)
    e = []
    for q in range(QCH):
        for d in range(1, nx):
            rcopy(gb.at[xsrcs[d], :, cols(q)], gb.at[xsrcs[d], :, cols(q)],
                  ssd.at[q, d], rsd.at[q, d], xpeers[d]).wait_recv()
        cp = rcopy(gb.at[:, :, cols(q)], ge.at[:, :, cols(q)], sse.at[q], rse.at[q], partner)
        cp.start()
        e.append(cp)
    for cp in bs + ds_:
        cp.wait_send()
    for q in range(QCH):
        e[q].wait()
        for j in range(nx):
            o_ref[pl.ds(pl.multiple_of(mine + j * blk, 8), blk), cols(q)] = gb[j, :, cols(q)]
            o_ref[pl.ds(pl.multiple_of(other + j * blk, 8), blk), cols(q)] = ge[j, :, cols(q)]


def _fused_kernel(nf, nr, rh, cw, design_hbm, lab, x0, dual_hbm, cz_hbm, prm,
                  ox, ot, pbuf, mbuf, rbuf, sbuf, design, dual, cz, lsem, *scratch):
    loads = [pltpu.make_async_copy(src, dst, lsem.at[i])
             for i, (src, dst) in enumerate([(design_hbm, design), (dual_hbm, dual), (cz_hbm, cz)])]
    for cp in loads:
        cp.start()
    feat_scr = scratch[:12]
    rows_scr = scratch[12:]
    nx = nr // 4

    me_f = lax.axis_index("feat")
    r = lax.axis_index("rows")
    fpeers = [lax.rem(me_f + d, nf) for d in range(1, nf)]
    c = lax.rem(r, 2)
    xi = lax.rem(r // 2, nx)
    rpeers = [r + 1 - 2 * c, lax.rem(r + 2 * nx, nr)]
    rpeers += [r - 2 * xi + 2 * lax.rem(xi + d, nx) for d in range(1, nx)]

    barrier = pltpu.get_barrier_semaphore()
    for p in fpeers:
        pl.semaphore_signal(barrier, inc=1, device_id=_device("feat", p), device_id_type=MESH)
    for p in rpeers:
        pl.semaphore_signal(barrier, inc=1, device_id=_device("rows", p), device_id_type=MESH)

    eta = prm[:, 0:1]
    rho = prm[:, 1:2]
    ox[...] = x0[...]
    ntile = design.shape[1] // TILE
    loads[0].wait()
    for turn in range(2):
        def margin_body(k, acc):
            cols = pl.ds(pl.multiple_of(k * TILE, TILE), TILE)
            xk = ox[:, cols].astype(jnp.bfloat16)
            return acc + lax.dot_general(
                xk, design[:, cols], (((1,), (1,)), ((), ())),
                preferred_element_type=jnp.float32)

        if turn == 0:
            pbuf[...] = lax.fori_loop(0, ntile, margin_body, jnp.zeros(pbuf.shape, jnp.float32), unroll=True)
        if turn == 0:
            pl.semaphore_wait(barrier, len(fpeers) + len(rpeers))
        _feat_allreduce(nf, rh, cw, pbuf, mbuf, *feat_scr[turn * 6:(turn + 1) * 6])
        sign = lab[...].astype(jnp.float32)
        rbuf[...] = (sign * jax.nn.sigmoid(-sign * mbuf[...])).astype(jnp.bfloat16)
        if turn == 0:
            loads[1].wait()
            loads[2].wait()

        def grad_body(j, carry):
            cols = pl.ds(pl.multiple_of(j * TILE, TILE), TILE)
            g = jnp.dot(rbuf[...], design[:, cols], preferred_element_type=jnp.float32)
            x = ox[:, cols]
            x = x - eta * (rho * (x - cz[:, cols] + dual[:, cols]) - g)
            ox[:, cols] = x
            if turn == 0:
                nxt = carry + lax.dot_general(
                    x.astype(jnp.bfloat16), design[:, cols], (((1,), (1,)), ((), ())),
                    preferred_element_type=jnp.float32)
            if turn == 1:
                sbuf[:, cols] = x + dual[:, cols]
                half = x.shape[0] // 2
                other = pl.multiple_of((1 - lax.rem(r, 2)) * half, 8)
                per = QCH // ntile
                wq = sbuf.shape[1] // QCH
                for h in range(per):
                    q = j * per + h
                    cq = pl.ds(pl.multiple_of(q * wq, 128), wq)
                    _rcopy("rows", sbuf.at[pl.ds(other, half), cq], rows_scr[0].at[:, cq],
                           rows_scr[6].at[q], rows_scr[7].at[q], rpeers[0]).start()
                nxt = carry
            return nxt

        if turn == 0:
            pbuf[...] = lax.fori_loop(0, ntile, grad_body, jnp.zeros(pbuf.shape, jnp.float32), unroll=True)
        else:
            lax.fori_loop(0, ntile, grad_body, 0, unroll=True)

    _rows_allreduce(nx, sbuf, ot, *rows_scr)


def _final_kernel(nr, x, total, dual, prm, ox, oz, ou):
    lim = prm[:, 2:3]
    mean = total[...] / nr
    new_z = mean - jnp.clip(mean, -lim, lim)
    ox[...] = x[...]
    oz[...] = new_z
    ou[...] = dual[...] + x[...] - new_z


def _fused(n_rows, n_feat, design, labels, x0, dual, cz, prm):
    k, width = x0.shape
    s = design.shape[0]
    rblocks = min(k // 8, n_feat)
    rh, cw = k // rblocks, s * rblocks // n_feat
    nx = n_rows // 4
    half, blk = k // 2, k // (2 * nx)
    f32 = jnp.float32
    dma = pltpu.SemaphoreType.DMA
    feat_scr = []
    for _ in range(2):
        feat_scr += [pltpu.VMEM((n_feat, rh, cw), f32), pltpu.VMEM((n_feat, rh, cw), f32)]
        feat_scr += [dma((n_feat,)) for _ in range(4)]
    rows_scr = [
        pltpu.VMEM((half, width), f32),
        pltpu.VMEM((half, width), f32),
        pltpu.VMEM((nx, blk, width), f32),
        pltpu.VMEM((blk, width), f32),
        pltpu.VMEM((nx, blk, width), f32),
        pltpu.VMEM((nx, blk, width), f32),
        dma((QCH,)), dma((QCH,)), dma((QCH, nx)), dma((QCH, nx)), dma((QCH,)), dma((QCH,)),
        dma((QCH, nx)), dma((QCH, nx)), dma((QCH,)), dma((QCH,)),
    ]
    vmem = pl.BlockSpec(memory_space=pltpu.VMEM)
    hbm = pl.BlockSpec(memory_space=pl.ANY)
    out = jax.ShapeDtypeStruct((k, width), f32)
    x, total = pl.pallas_call(
        functools.partial(_fused_kernel, n_feat, n_rows, rh, cw),
        out_shape=(out, out),
        in_specs=[hbm, vmem, vmem, hbm, hbm, vmem],
        out_specs=(vmem, vmem),
        scratch_shapes=[
            pltpu.VMEM((k, s), f32),
            pltpu.VMEM((k, s), f32),
            pltpu.VMEM((k, s), jnp.bfloat16),
            pltpu.VMEM((k, width), f32),
            pltpu.VMEM(design.shape, design.dtype),
            pltpu.VMEM((k, width), f32),
            pltpu.VMEM((k, width), f32),
            dma((3,)),
        ] + feat_scr + rows_scr,
        compiler_params=pltpu.CompilerParams(
            collective_id=0, has_side_effects=True, vmem_limit_bytes=60 * 1024 * 1024),
    )(design, labels, x0, dual, cz, prm)
    tile = pl.BlockSpec((k, 2 * TILE), lambda j: (0, j))
    return pl.pallas_call(
        functools.partial(_final_kernel, n_rows),
        out_shape=(out, out, out),
        grid=(width // (2 * TILE),),
        in_specs=[tile, tile, tile, pl.BlockSpec(prm.shape, lambda j: (0, 0))],
        out_specs=(tile, tile, tile),
    )(x, total, dual, prm)


def per_device(n_rows, n_feat, design, labels, local_x, dual_u, consensus_z, step_size, rho, penalty):
    prm = jnp.stack([step_size, rho, penalty / (rho * n_rows)], axis=1)
    x, new_z, new_u = _fused(n_rows, n_feat, design, labels, local_x[0], dual_u[0],
                             consensus_z, prm)
    return (x[None], new_z, new_u[None])


def solution(mesh):
    in_specs = (
        P("rows", "feat"),
        P(None, "rows"),
        P("rows", None, "feat"),
        P("rows", None, "feat"),
        P(None, "feat"),
        P(),
        P(),
        P(),
    )
    out_specs = (P("rows", None, "feat"), P(None, "feat"), P("rows", None, "feat"))
    fn = functools.partial(per_device, mesh.shape["rows"], mesh.shape["feat"])
    return jax.shard_map(
        fn, mesh=mesh, in_specs=in_specs, out_specs=out_specs, check_vma=False
    )
```

```python
import functools

import jax
import jax.numpy as jnp
from jax import lax
from jax.experimental import pallas as pl
from jax.experimental.pallas import tpu as pltpu
from jax.sharding import PartitionSpec as P

MESH = pl.DeviceIdType.MESH
AXES = ("rows", "feat")
TILE = 1024
QCH = 16


def _device(axis, peer):
    return tuple(peer if a == axis else lax.axis_index(a) for a in AXES)


def _rcopy(axis, src, dst, ss, rs, p):
    return pltpu.make_async_remote_copy(
        src_ref=src, dst_ref=dst, send_sem=ss, recv_sem=rs,
        device_id=_device(axis, p), device_id_type=MESH)


def _feat_allreduce(n, rh, cw, x_ref, o_ref, recv, gath, ss1, rs1, ss2, rs2):
    me = lax.axis_index("feat")
    peers = [lax.rem(me + d, n) for d in range(n)]
    srcs = [lax.rem(me + n - d, n) for d in range(n)]
    cblocks = x_ref.shape[1] // cw

    def block(ref, p):
        r = pl.multiple_of((p // cblocks) * rh, 8)
        c = pl.multiple_of((p % cblocks) * cw, 128)
        return ref.at[pl.ds(r, rh), pl.ds(c, cw)]

    sends = []
    for d in range(1, n):
        c = _rcopy("feat", block(x_ref, peers[d]), recv.at[me], ss1.at[d], rs1.at[d], peers[d])
        c.start()
        sends.append(c)
    acc = block(x_ref, me)[...]
    for d in range(1, n):
        _rcopy("feat", recv.at[srcs[d]], recv.at[srcs[d]], ss1.at[d], rs1.at[d], srcs[d]).wait_recv()
        acc = acc + recv[srcs[d]]
    gath[me] = acc
    sends2 = []
    for d in range(1, n):
        c = _rcopy("feat", gath.at[me], gath.at[me], ss2.at[d], rs2.at[d], peers[d])
        c.start()
        sends2.append(c)
    for c in sends:
        c.wait_send()
    for d in range(1, n):
        _rcopy("feat", gath.at[srcs[d]], gath.at[srcs[d]], ss2.at[d], rs2.at[d], srcs[d]).wait_recv()
    for c in sends2:
        c.wait_send()
    for p in range(n):
        r, c = (p // cblocks) * rh, (p % cblocks) * cw
        o_ref[r:r + rh, c:c + cw] = gath[p]


def _rows_allreduce(nx, x_ref, o_ref, ra, hbuf, rb, rc, gb, ge,
                    ssa, rsa, ssb, rsb, ssc, rsc, ssd, rsd, sse, rse):
    r = lax.axis_index("rows")
    n = 4 * nx
    half, blk = x_ref.shape[0] // 2, x_ref.shape[0] // (2 * nx)
    wq = x_ref.shape[1] // QCH
    c = lax.rem(r, 2)
    xi = lax.rem(r // 2, nx)
    base = r - 2 * xi
    partner = r + 1 - 2 * c
    xpeers = [base + 2 * lax.rem(xi + d, nx) for d in range(nx)]
    xsrcs = [lax.rem(xi + nx - d, nx) for d in range(nx)]
    zpeer = lax.rem(r + 2 * nx, n)
    rcopy = functools.partial(_rcopy, "rows")
    mine = pl.multiple_of(c * half, 8)
    other = pl.multiple_of((1 - c) * half, 8)

    def cols(q):
        return pl.ds(q * wq, wq)

    def rows_of(j):
        return pl.ds(pl.multiple_of(j * blk, 8), blk)

    a = [rcopy(x_ref.at[pl.ds(other, half), cols(q)], ra.at[:, cols(q)], ssa.at[q], rsa.at[q], partner)
         for q in range(QCH)]
    bs = []
    for q in range(QCH):
        a[q].wait()
        hbuf[:, cols(q)] = x_ref[pl.ds(mine, half), cols(q)] + ra[:, cols(q)]
        for d in range(1, nx):
            j = lax.rem(xi + d, nx)
            cp = rcopy(hbuf.at[rows_of(j), cols(q)], rb.at[xi, :, cols(q)],
                       ssb.at[q, d], rsb.at[q, d], xpeers[d])
            cp.start()
            bs.append(cp)
    cz = []
    for q in range(QCH):
        acc = hbuf[rows_of(xi), cols(q)]
        for d in range(1, nx):
            rcopy(rb.at[xsrcs[d], :, cols(q)], rb.at[xsrcs[d], :, cols(q)],
                  ssb.at[q, d], rsb.at[q, d], xpeers[d]).wait_recv()
            acc = acc + rb[xsrcs[d], :, cols(q)]
        gb[xi, :, cols(q)] = acc
        cp = rcopy(gb.at[xi, :, cols(q)], rc.at[:, cols(q)], ssc.at[q], rsc.at[q], zpeer)
        cp.start()
        cz.append(cp)
    ds_ = []
    for q in range(QCH):
        cz[q].wait()
        gb[xi, :, cols(q)] = gb[xi, :, cols(q)] + rc[:, cols(q)]
        for d in range(1, nx):
            cp = rcopy(gb.at[xi, :, cols(q)], gb.at[xi, :, cols(q)], ssd.at[q, d], rsd.at[q, d], xpeers[d])
            cp.start()
            ds_.append(cp)
    e = []
    for q in range(QCH):
        for d in range(1, nx):
            rcopy(gb.at[xsrcs[d], :, cols(q)], gb.at[xsrcs[d], :, cols(q)],
                  ssd.at[q, d], rsd.at[q, d], xpeers[d]).wait_recv()
        cp = rcopy(gb.at[:, :, cols(q)], ge.at[:, :, cols(q)], sse.at[q], rse.at[q], partner)
        cp.start()
        e.append(cp)
    for cp in bs + ds_:
        cp.wait_send()
    for q in range(QCH):
        e[q].wait()
        for j in range(nx):
            o_ref[pl.ds(pl.multiple_of(mine + j * blk, 8), blk), cols(q)] = gb[j, :, cols(q)]
            o_ref[pl.ds(pl.multiple_of(other + j * blk, 8), blk), cols(q)] = ge[j, :, cols(q)]


def _fused_kernel(nf, nr, rh, cw, design_hbm, lab, x0, dual_hbm, cz_hbm, prm,
                  ox, ot, pbuf, mbuf, rbuf, sbuf, design, dual, cz, lsem, *scratch):
    loads = [pltpu.make_async_copy(src, dst, lsem.at[i])
             for i, (src, dst) in enumerate([(design_hbm, design), (dual_hbm, dual), (cz_hbm, cz)])]
    for cp in loads:
        cp.start()
    feat_scr = scratch[:12]
    rows_scr = scratch[12:]
    nx = nr // 4

    me_f = lax.axis_index("feat")
    r = lax.axis_index("rows")
    fpeers = [lax.rem(me_f + d, nf) for d in range(1, nf)]
    c = lax.rem(r, 2)
    xi = lax.rem(r // 2, nx)
    rpeers = [r + 1 - 2 * c, lax.rem(r + 2 * nx, nr)]
    rpeers += [r - 2 * xi + 2 * lax.rem(xi + d, nx) for d in range(1, nx)]

    barrier = pltpu.get_barrier_semaphore()
    for p in fpeers:
        pl.semaphore_signal(barrier, inc=1, device_id=_device("feat", p), device_id_type=MESH)
    for p in rpeers:
        pl.semaphore_signal(barrier, inc=1, device_id=_device("rows", p), device_id_type=MESH)

    eta = prm[:, 0:1]
    rho = prm[:, 1:2]
    ox[...] = x0[...]
    ntile = design.shape[1] // TILE
    loads[0].wait()
    for turn in range(2):
        def margin_body(k, acc):
            cols = pl.ds(pl.multiple_of(k * TILE, TILE), TILE)
            xk = ox[:, cols].astype(jnp.bfloat16)
            return acc + lax.dot_general(
                xk, design[:, cols], (((1,), (1,)), ((), ())),
                preferred_element_type=jnp.float32)

        if turn == 0:
            pbuf[...] = lax.fori_loop(0, ntile, margin_body, jnp.zeros(pbuf.shape, jnp.float32), unroll=True)
        if turn == 0:
            pl.semaphore_wait(barrier, len(fpeers) + len(rpeers))
        _feat_allreduce(nf, rh, cw, pbuf, mbuf, *feat_scr[turn * 6:(turn + 1) * 6])
        sign = lab[...].astype(jnp.float32)
        rbuf[...] = (sign * jax.nn.sigmoid(-sign * mbuf[...])).astype(jnp.bfloat16)
        if turn == 0:
            loads[1].wait()
            loads[2].wait()

        def grad_body(j, carry):
            cols = pl.ds(pl.multiple_of(j * TILE, TILE), TILE)
            g = jnp.dot(rbuf[...], design[:, cols], preferred_element_type=jnp.float32)
            x = ox[:, cols]
            x = x - eta * (rho * (x - cz[:, cols] + dual[:, cols]) - g)
            ox[:, cols] = x
            if turn == 0:
                nxt = carry + lax.dot_general(
                    x.astype(jnp.bfloat16), design[:, cols], (((1,), (1,)), ((), ())),
                    preferred_element_type=jnp.float32)
            if turn == 1:
                sbuf[:, cols] = x + dual[:, cols]
                half = x.shape[0] // 2
                other = pl.multiple_of((1 - lax.rem(r, 2)) * half, 8)
                per = QCH // ntile
                wq = sbuf.shape[1] // QCH
                for h in range(per):
                    q = j * per + h
                    cq = pl.ds(pl.multiple_of(q * wq, 128), wq)
                    _rcopy("rows", sbuf.at[pl.ds(other, half), cq], rows_scr[0].at[:, cq],
                           rows_scr[6].at[q], rows_scr[7].at[q], rpeers[0]).start()
                nxt = carry
            return nxt

        if turn == 0:
            pbuf[...] = lax.fori_loop(0, ntile, grad_body, jnp.zeros(pbuf.shape, jnp.float32), unroll=True)
        else:
            lax.fori_loop(0, ntile, grad_body, 0, unroll=True)

    _rows_allreduce(nx, sbuf, ot, *rows_scr)


def _final_kernel(nr, x, total, dual, prm, ox, oz, ou):
    lim = prm[:, 2:3]
    mean = total[...] / nr
    new_z = mean - jnp.clip(mean, -lim, lim)
    ox[...] = x[...]
    oz[...] = new_z
    ou[...] = dual[...] + x[...] - new_z


def _fused(n_rows, n_feat, design, labels, x0, dual, cz, prm):
    k, width = x0.shape
    s = design.shape[0]
    rblocks = min(k // 8, n_feat)
    rh, cw = k // rblocks, s * rblocks // n_feat
    nx = n_rows // 4
    half, blk = k // 2, k // (2 * nx)
    f32 = jnp.float32
    dma = pltpu.SemaphoreType.DMA
    feat_scr = []
    for _ in range(2):
        feat_scr += [pltpu.VMEM((n_feat, rh, cw), f32), pltpu.VMEM((n_feat, rh, cw), f32)]
        feat_scr += [dma((n_feat,)) for _ in range(4)]
    rows_scr = [
        pltpu.VMEM((half, width), f32),
        pltpu.VMEM((half, width), f32),
        pltpu.VMEM((nx, blk, width), f32),
        pltpu.VMEM((blk, width), f32),
        pltpu.VMEM((nx, blk, width), f32),
        pltpu.VMEM((nx, blk, width), f32),
        dma((QCH,)), dma((QCH,)), dma((QCH, nx)), dma((QCH, nx)), dma((QCH,)), dma((QCH,)),
        dma((QCH, nx)), dma((QCH, nx)), dma((QCH,)), dma((QCH,)),
    ]
    vmem = pl.BlockSpec(memory_space=pltpu.VMEM)
    hbm = pl.BlockSpec(memory_space=pl.ANY)
    out = jax.ShapeDtypeStruct((k, width), f32)
    x, total = pl.pallas_call(
        functools.partial(_fused_kernel, n_feat, n_rows, rh, cw),
        out_shape=(out, out),
        in_specs=[hbm, vmem, vmem, hbm, hbm, vmem],
        out_specs=(vmem, vmem),
        scratch_shapes=[
            pltpu.VMEM((k, s), f32),
            pltpu.VMEM((k, s), f32),
            pltpu.VMEM((k, s), jnp.bfloat16),
            pltpu.VMEM((k, width), f32),
            pltpu.VMEM(design.shape, design.dtype),
            pltpu.VMEM((k, width), f32),
            pltpu.VMEM((k, width), f32),
            dma((3,)),
        ] + feat_scr + rows_scr,
        compiler_params=pltpu.CompilerParams(
            collective_id=0, has_side_effects=True, vmem_limit_bytes=60 * 1024 * 1024),
    )(design, labels, x0, dual, cz, prm)
    tile = pl.BlockSpec((k, 2 * TILE), lambda j: (0, j))
    return pl.pallas_call(
        functools.partial(_final_kernel, n_rows),
        out_shape=(out, out, out),
        grid=(width // (2 * TILE),),
        in_specs=[tile, tile, tile, pl.BlockSpec(prm.shape, lambda j: (0, 0))],
        out_specs=(tile, tile, tile),
    )(x, total, dual, prm)


def per_device(n_rows, n_feat, design, labels, local_x, dual_u, consensus_z, step_size, rho, penalty):
    prm = jnp.stack([step_size, rho, penalty / (rho * n_rows)], axis=1)
    x, new_z, new_u = _fused(n_rows, n_feat, design, labels, local_x[0], dual_u[0],
                             consensus_z, prm)
    return (x[None], new_z, new_u[None])


def solution(mesh):
    in_specs = (
        P("rows", "feat"),
        P(None, "rows"),
        P("rows", None, "feat"),
        P("rows", None, "feat"),
        P(None, "feat"),
        P(),
        P(),
        P(),
    )
    out_specs = (P("rows", None, "feat"), P(None, "feat"), P("rows", None, "feat"))
    fn = functools.partial(per_device, mesh.shape["rows"], mesh.shape["feat"])
    return jax.shard_map(
        fn, mesh=mesh, in_specs=in_specs, out_specs=out_specs, check_vma=False
    )
```
